256 devices in a mesh: dp: 4 (over x), vocab: 64 (over y, z, core).
Axes of the slice: x: 4, y: 4, z: 8, core: 2. Of those that a mesh axis runs over, the one named last changes fastest.
Arguments:
- teacher_hidden: bfloat16 [1024, 8192], P('dp', 'vocab'), may hold values from -200 to 200
- student_hidden: bfloat16 [1024, 3584], P('dp', 'vocab'), may hold values from -200 to 200
- teacher_head: bfloat16 [8192, 81920], P('dp', 'vocab'), may hold values from -0.0625 to 0.0625
- student_head: bfloat16 [3584, 81920], P('dp', 'vocab'), may hold values from -0.09375 to 0.09375
- allowed: int32 [1024, 640], P('dp', 'vocab'), may hold values from 0 to 1, as said below
- sampled: int32 [1024], P('dp'), may hold values from 0 to 81919, as said below
Outputs:
- row_kl: float32 [1024], P('dp')
- sampled_logprob: float32 [1024], P('dp')
- head_grad: float32 [3584, 81920], P('dp', 'vocab')
The draws below stay inside these ranges and needn't reach their ends.
Inputs may be any that keep to these rules, and one draw needn't show every extreme that they name: allowed is 0 or 1; the block of every row's sampled token is allowed, so every row has an allowed block; the share of allowed blocks differs from block to block. sampled[r] lies in a block that allowed marks for row r.
All inputs are finite; a program needn't handle non-finite values.
Results may differ from the reference program's by a relative error of at most 0.004.
Values may be sent and summed in bfloat16 or wider, within the bound.
No kernel may reach another device: no remote copies, remote signals or barrier semaphores. Data moves between devices by JAX's collectives and lax.ppermute only.
A program may use at most 128 MiB of HBM per device.

```python
import jax
import jax.numpy as jnp

DT = 8192
DS = 3584
BLOCK = 128
TOKENS = 1024
NB = 640
VOCAB = 81920


def hidden_draw(key, shape):
    first_key = jax.random.fold_in(key, 0)
    noise = jnp.clip(jax.random.normal(first_key, shape, jnp.float32), -4.0, 4.0)
    values = 4.0 * noise
    return values.astype(jnp.bfloat16)


def draw_teacher_hidden(key, part):
    return hidden_draw(jax.random.fold_in(key, 11), (TOKENS, DT))


def draw_student_hidden(key, part):
    return hidden_draw(jax.random.fold_in(key, 23), (TOKENS, DS))


def grammar_draw(key):
    rate_key, bits_key, block_key, offset_key = jax.random.split(jax.random.fold_in(key, 37), 4)
    block_rate = jax.random.randint(rate_key, (NB,), 1, 13)
    bits = jax.random.randint(bits_key, (TOKENS, NB), 0, 64) < block_rate[None, :]
    chosen = jax.random.randint(block_key, (TOKENS,), 0, NB)
    columns = jnp.arange(NB, dtype=jnp.int32)
    bits = jnp.logical_or(bits, columns[None, :] == chosen[:, None])
    tokens_drawn = chosen * BLOCK + jax.random.randint(offset_key, (TOKENS,), 0, BLOCK)
    return (bits.astype(jnp.int32), tokens_drawn.astype(jnp.int32))


def draw_allowed(key, part):
    return grammar_draw(key)[0]


def draw_sampled(key, part):
    return grammar_draw(key)[1]


def shard_levels(own_key, extent, shards, smallest, top_value):
    def one(dim, blocks):
        steps = jax.random.uniform(jax.random.fold_in(jax.random.fold_in(own_key, 6), dim), (blocks,), jnp.float32, smallest / len(shards), top_value / len(shards))
        return jnp.repeat(jnp.exp(steps), extent[dim] // blocks).reshape((-1,) + (1,) * (len(extent) - dim - 1))

    loudness = one(*shards[0])
    for cut in shards[1:]:
        loudness = loudness * one(*cut)
    return loudness


def normal_values(key, extent, deviation, most, cuts=(), kind=jnp.bfloat16):
    drawn = jax.random.normal(key, extent, jnp.float32) * deviation
    if len(cuts) > 0:
        drawn = shard_levels(key, extent, cuts, -0.22, 0.18) * drawn
    return jnp.clip(drawn, min=-most, max=most).astype(kind)


def setup_inputs(seed: int = 0) -> dict:
    arg_keys = jax.random.split(jax.random.key(seed), 7)
    return {
        "teacher_hidden": draw_teacher_hidden(jax.random.fold_in(arg_keys[6], 71), 0),
        "student_hidden": draw_student_hidden(jax.random.fold_in(arg_keys[6], 71), 0),
        "teacher_head": normal_values(arg_keys[2], (DT, VOCAB), DT ** -0.5, 0.0625, ((0, 4), (1, 64))),
        "student_head": normal_values(arg_keys[3], (DS, VOCAB), DS ** -0.5, 0.09375, ((0, 4), (1, 64))),
        "allowed": draw_allowed(jax.random.fold_in(arg_keys[6], 71), 0),
        "sampled": draw_sampled(jax.random.fold_in(arg_keys[6], 71), 0),
    }


negative_fill = -1.0e30


def reference(teacher_hidden, student_hidden, teacher_head, student_head, allowed, sampled):
    teacher_logits = jnp.dot(teacher_hidden, teacher_head, preferred_element_type=jnp.float32)
    student_logits = jnp.dot(student_hidden, student_head, preferred_element_type=jnp.float32)
    permitted = jnp.repeat(allowed, BLOCK, axis=1)
    is_open = permitted > 0
    teacher_masked = jnp.where(is_open, teacher_logits, negative_fill)
    student_masked = jnp.where(is_open, student_logits, negative_fill)
    top_teacher = jnp.max(teacher_masked, axis=1)
    top_student = jnp.max(student_masked, axis=1)
    exp_teacher = jnp.where(is_open, jnp.exp(teacher_masked - top_teacher[:, None]), jnp.float32(0.0))
    exp_student = jnp.where(is_open, jnp.exp(student_masked - top_student[:, None]), jnp.float32(0.0))
    sum_teacher = jnp.sum(exp_teacher, axis=1)
    sum_student = jnp.sum(exp_student, axis=1)
    cross = jnp.sum(exp_teacher * (teacher_logits - student_logits), axis=1)
    vocab_ids = jnp.arange(VOCAB, dtype=jnp.int32)
    picked = jnp.sum(jnp.where(vocab_ids[None, :] == sampled[:, None], student_logits, jnp.float32(0.0)), axis=1)
    log_teacher = top_teacher + jnp.log(sum_teacher)
    log_student = top_student + jnp.log(sum_student)
    row_kl = cross / sum_teacher - log_teacher + log_student
    sampled_logprob = picked - log_student
    grad_logits = (exp_student / sum_student[:, None] - exp_teacher / sum_teacher[:, None]).astype(jnp.bfloat16)
    head_grad = jnp.dot(student_hidden.T, grad_logits, preferred_element_type=jnp.float32)
    return row_kl, sampled_logprob, head_grad
```

```python
import functools

import jax
import jax.numpy as jnp
from jax import lax
from jax.experimental import pallas as pl
from jax.experimental.pallas import tpu as pltpu
from jax.sharding import Mesh
from jax.sharding import PartitionSpec as P

CAP = 80
NEG = -1e30
BLOCK = 128
LOCAL = ("y", "z", "c")


def dot(a, b, dims):
    return lax.dot_general(a, b, (dims, ((), ())), preferred_element_type=jnp.float32)


def params(**kw):
    return pltpu.CompilerParams(vmem_limit_bytes=48 << 20, **kw)


def selector(pos_row):
    lines = lax.broadcasted_iota(jnp.int32, (CAP, pos_row.shape[-1]), 0)
    return lines == pos_row


def partial_kernel(pos, teach, stud, head_t, head_s, out, kept, sel, rows_t, rows_s):
    count, chunks = teach.shape[0], teach.shape[1]
    blocks = kept_blocks = sel.shape[0] // CAP
    b = pl.program_id(0)

    @pl.when(b == 0)
    def _():
        for i in range(count):
            for k in range(kept_blocks):
                sel[k * CAP : (k + 1) * CAP, :] = selector(pos[i, k : k + 1, :]).astype(
                    jnp.float32
                ).astype(jnp.bfloat16)
            marks = sel[...]
            if chunks % 2 == 0:
                for k in range(chunks // 2):
                    pair = jnp.concatenate([teach[i, 2 * k], teach[i, 2 * k + 1]], axis=1)
                    rows_t[i, :, k * 256 : (k + 1) * 256] = dot(marks, pair, ((1,), (0,))).astype(
                        jnp.bfloat16
                    )
            else:
                for k in range(chunks):
                    rows_t[i, :, k * 128 : (k + 1) * 128] = dot(
                        marks, teach[i, k], ((1,), (0,))
                    ).astype(jnp.bfloat16)
            rows_s[i] = dot(marks, stud[i], ((1,), (1,))).astype(jnp.bfloat16)

    del blocks
    here = pl.ds(pl.multiple_of(b * CAP, 16), CAP)
    for i in range(count):
        mine = rows_s[i, here, :]
        out[i, 0, 0] = dot(rows_t[i, here, :], head_t[...], ((1,), (0,)))
        out[i, 1, 0] = dot(mine, head_s[...], ((1,), (0,)))
        kept[i, 0] = mine


def partial_logits(pos, teach, stud, head_t, head_s):
    count, chunks, tokens, _ = teach.shape
    deep_t, width = head_t.shape
    deep_s = head_s.shape[0]
    blocks = width // BLOCK
    whole = lambda a: pl.BlockSpec(a.shape, lambda b: (0,) * a.ndim)
    return pl.pallas_call(
        partial_kernel,
        name="partial_logits",
        grid=(blocks,),
        in_specs=[
            whole(pos),
            whole(teach),
            whole(stud),
            pl.BlockSpec((deep_t, BLOCK), lambda b: (0, b)),
            pl.BlockSpec((deep_s, BLOCK), lambda b: (0, b)),
        ],
        out_specs=[
            pl.BlockSpec((count, 2, 1, CAP, BLOCK), lambda b: (0, 0, b, 0, 0)),
            pl.BlockSpec((count, 1, CAP, deep_s), lambda b: (0, b, 0, 0)),
        ],
        out_shape=[
            jax.ShapeDtypeStruct((count, 2, blocks, CAP, BLOCK), jnp.float32),
            jax.ShapeDtypeStruct((count, blocks, CAP, deep_s), jnp.bfloat16),
        ],
        scratch_shapes=[
            pltpu.VMEM((blocks * CAP, tokens), jnp.bfloat16),
            pltpu.VMEM((count, blocks * CAP, deep_t), jnp.bfloat16),
            pltpu.VMEM((count, blocks * CAP, deep_s), jnp.bfloat16),
        ],
        compiler_params=params(),
        cost_estimate=pl.CostEstimate(
            flops=4 * count * blocks * CAP * (deep_t + deep_s) * tokens,
            bytes_accessed=2 * (deep_t + deep_s) * (width + count * tokens),
            transcendentals=0,
        ),
    )(pos, teach, stud, head_t, head_s)


def spread(mark, line):
    return jnp.sum(jnp.where(mark, line, jnp.zeros_like(line)), axis=1, keepdims=True)


def fold(mark, column):
    return jnp.sum(jnp.where(mark, column, jnp.zeros_like(column)), axis=0, keepdims=True)


def stats_kernel(pos, target, a0, a1, a2, a3, logits, stats):
    blocks = logits.shape[1]
    tokens = pos.shape[-1]
    tops = [jnp.full((1, tokens), NEG, jnp.float32) for _ in range(2)]
    for b in range(blocks):
        mark = selector(pos[b : b + 1, :])
        for h in range(2):
            total = (a0[0, h, b] + a1[0, h, b]) + (a2[0, h, b] + a3[0, h, b])
            logits[h, b] = total
            peak = jnp.max(total, axis=1, keepdims=True)
            tops[h] = jnp.maximum(
                tops[h], jnp.max(jnp.where(mark, peak, NEG), axis=0, keepdims=True)
            )
    zero = jnp.zeros((1, tokens), jnp.float32)
    sum_t, cross, sum_s, picked = zero, zero, zero, zero
    lanes = lax.broadcasted_iota(jnp.int32, (CAP, BLOCK), 1)
    for b in range(blocks):
        mark = selector(pos[b : b + 1, :])
        lt, ls = logits[0, b], logits[1, b]
        et = jnp.exp(lt - spread(mark, tops[0]))
        es = jnp.exp(ls - spread(mark, tops[1]))
        wanted = spread(mark, target[...] - b * BLOCK)
        sum_t = sum_t + fold(mark, jnp.sum(et, axis=1, keepdims=True))
        cross = cross + fold(mark, jnp.sum(et * (lt - ls), axis=1, keepdims=True))
        sum_s = sum_s + fold(mark, jnp.sum(es, axis=1, keepdims=True))
        picked = picked + fold(
            mark, jnp.sum(jnp.where(lanes == wanted, ls, 0.0), axis=1, keepdims=True)
        )
    stats[...] = jnp.concatenate([tops[0], sum_t, cross, tops[1], sum_s, picked, zero, zero], axis=0)


def row_stats(pos, target, parts):
    blocks = parts[0].shape[2]
    return pl.pallas_call(
        stats_kernel,
        name="row_stats",
        out_shape=[
            jax.ShapeDtypeStruct((2, blocks, CAP, BLOCK), jnp.float32),
            jax.ShapeDtypeStruct((8, pos.shape[-1]), jnp.float32),
        ],
        compiler_params=params(),
    )(pos, target, *parts)


def combined(seen):
    top_t = jnp.max(seen[:, 0, :], axis=0, keepdims=True)
    top_s = jnp.max(seen[:, 3, :], axis=0, keepdims=True)
    scale_t = jnp.exp(seen[:, 0, :] - top_t)
    scale_s = jnp.exp(seen[:, 3, :] - top_s)
    total = lambda a: jnp.sum(a, axis=0, keepdims=True)
    sum_t = total(seen[:, 1, :] * scale_t)
    cross = total(seen[:, 2, :] * scale_t)
    sum_s = total(seen[:, 4, :] * scale_s)
    picked = total(seen[:, 5, :])
    log_t = top_t + jnp.log(sum_t)
    log_s = top_s + jnp.log(sum_s)
    return top_t, sum_t, top_s, sum_s, cross / sum_t - log_t + log_s, picked - log_s


def grad_kernel(pos, seen, logits, grad, rows):
    top_t, sum_t, top_s, sum_s, row_kl, logprob = combined(seen[...])
    zero = jnp.zeros_like(row_kl)
    rows[...] = jnp.concatenate([row_kl, logprob] + [zero] * 6, axis=0)
    inv_t, inv_s = 1.0 / sum_t, 1.0 / sum_s
    for b in range(logits.shape[1]):
        mark = selector(pos[b : b + 1, :])
        et = jnp.exp(logits[0, b] - spread(mark, top_t)) * spread(mark, inv_t)
        es = jnp.exp(logits[1, b] - spread(mark, top_s)) * spread(mark, inv_s)
        grad[b] = (es - et).astype(jnp.bfloat16)


def row_grads(pos, seen, logits):
    return pl.pallas_call(
        grad_kernel,
        name="row_grads",
        out_shape=[
            jax.ShapeDtypeStruct(logits.shape[1:], jnp.bfloat16),
            jax.ShapeDtypeStruct((8, pos.shape[-1]), jnp.float32),
        ],
        compiler_params=params(),
    )(pos, seen, logits)


def head_kernel(*refs):
    *inputs, out = refs
    half = len(inputs) // 2
    total = None
    for rows, grads in zip(inputs[:half], inputs[half:]):
        part = dot(rows[0, 0], grads[0], ((0,), (0,)))
        total = part if total is None else total + part
    out[...] = total


def head_gradient(rows, grads):
    deep = rows[0][0].shape[-1]
    blocks = grads[0].shape[0]
    return pl.pallas_call(
        head_kernel,
        name="head_gradient",
        grid=(blocks,),
        in_specs=[
            pl.BlockSpec((1, 1, CAP, deep), functools.partial(lambda i, b: (i, b, 0, 0), i))
            for _, i in rows
        ]
        + [pl.BlockSpec((1, CAP, BLOCK), lambda b: (b, 0, 0)) for _ in grads],
        out_specs=pl.BlockSpec((deep, BLOCK), lambda b: (0, b)),
        out_shape=jax.ShapeDtypeStruct((deep, blocks * BLOCK), jnp.float32),
        compiler_params=params(),
    )(*(array for array, _ in rows), *grads)


def build(sx, sz, sc):
    turn = lambda step: [
        (x * sx + y, ((y + step - x) % sx) * sx + y) for x in range(sx) for y in range(sx)
    ]
    spread_out = [(x * sx + y, y * sx + (x + y) % sx) for x in range(sx) for y in range(sx)]
    shift = lambda step: [(y, (y + step) % sx) for y in range(sx)]

    def to_owner(a, step):
        return lax.ppermute(a, ("x", "y"), turn(step))

    def both_cores(mine):
        if sc == 1:
            return mine[:, None]
        other = lax.ppermute(mine, "c", [(0, 1), (1, 0)])
        first = lax.axis_index("c") == 0
        return jnp.stack([jnp.where(first, mine, other), jnp.where(first, other, mine)], axis=1)

    def features(pay, tokens):
        full = both_cores(pay)
        chunks = full.shape[0] * full.shape[1]
        full = full.reshape(chunks, -1, BLOCK)
        teach = full[:, :tokens]
        stud = full[:, tokens:].reshape(chunks, tokens // BLOCK, -1, BLOCK)
        stud = stud.transpose(0, 2, 1, 3).reshape(-1, tokens)
        return teach, stud

    def neighbours(pay):
        after = lax.ppermute(pay, "y", shift(-1))
        before = lax.ppermute(pay, "y", shift(1))
        return after, before

    def opposite(after, before):
        half = after.shape[0] // 2
        if half == 0:
            return lax.ppermute(after, "y", shift(-1))
        low = lax.ppermute(after[:half], "y", shift(-1))
        high = lax.ppermute(before[half:], "y", shift(1))
        return jnp.concatenate([low, high], axis=0)

    def everyone(stats):
        copies = jnp.broadcast_to(stats[None], (sx * sz * sc, *stats.shape))
        return lax.all_to_all(copies, LOCAL, split_axis=0, concat_axis=0, tiled=True)

    def compact(pay, head_t, head_s, allowed, target, places, own_pos):
        tokens = own_pos.shape[-1]
        after, before = neighbours(pay)
        teach, stud = features(pay, tokens)
        part0, kept0 = partial_logits(places[0][None], teach[None], stud[None], head_t, head_s)
        got = [to_owner(part0, 0)]
        far = opposite(after, before)
        pairs = [features(after, tokens), features(before, tokens)]
        kept = [(kept0, 0)]
        for step, (teach, stud) in zip((1, 3), pairs):
            part, hold = partial_logits(places[step][None], teach[None], stud[None], head_t, head_s)
            got.append(to_owner(part, step))
            kept.append((hold, 0))
        teach, stud = features(far, tokens)
        part, hold = partial_logits(places[2][None], teach[None], stud[None], head_t, head_s)
        got.append(to_owner(part, 2))
        kept.append((hold, 0))
        logits, stats = row_stats(own_pos, target[None], got)
        grad, rows = row_grads(own_pos, everyone(stats), logits)
        grads = [to_owner(grad, step) for step in (0, 1, 3, 2)]
        return rows[0], rows[1], head_gradient(kept, grads)

    def dense(pay, head_t, head_s, allowed, target, places, own_pos):
        tokens, blocks = allowed.shape
        width = head_t.shape[1]
        after, before = neighbours(pay)
        pays = {0: pay, 1: after, 3: before, 2: opposite(after, before)}
        studs, total = {}, 0.0
        for step in range(sx):
            teach, stud = features(pays[step], tokens)
            studs[step] = stud
            teach = teach.transpose(1, 0, 2).reshape(tokens, -1)
            part = jnp.concatenate(
                [dot(teach, head_t, ((1,), (0,))), dot(stud, head_s, ((0,), (0,)))], axis=1
            )
            total = total + to_owner(part, step)
        lt, ls = total[:, :width], total[:, width:]
        open_ = jnp.broadcast_to((allowed > 0)[:, :, None], (tokens, blocks, BLOCK))
        open_ = open_.reshape(tokens, width)
        ids = jnp.arange(width, dtype=jnp.int32)
        picked = jnp.sum(jnp.where(ids[None, :] == target[:, None], ls, 0.0), axis=1)
        top_t = jnp.max(jnp.where(open_, lt, NEG), axis=1)
        top_s = jnp.max(jnp.where(open_, ls, NEG), axis=1)
        et = jnp.where(open_, jnp.exp(jnp.where(open_, lt, NEG) - top_t[:, None]), 0.0)
        es = jnp.where(open_, jnp.exp(jnp.where(open_, ls, NEG) - top_s[:, None]), 0.0)
        lines = [top_t, et.sum(1), (et * (lt - ls)).sum(1), top_s, es.sum(1), picked]
        stats = jnp.stack(lines + [jnp.zeros_like(top_t)] * 2)
        all_t, sum_t, all_s, sum_s, row_kl, logprob = combined(everyone(stats))
        scale_t = (jnp.exp(top_t[None] - all_t) / sum_t)[0]
        scale_s = (jnp.exp(top_s[None] - all_s) / sum_s)[0]
        grad = (es * scale_s[:, None] - et * scale_t[:, None]).astype(jnp.bfloat16)
        head = sum(
            dot(studs[step], to_owner(grad, step), ((1,), (0,))) for step in range(sx)
        )
        return row_kl[0], logprob[0], head

    def per_device(teacher_hidden, student_hidden, head_t, head_s, allowed, sampled):
        tokens, blocks = allowed.shape
        width = head_t.shape[1]
        stud = student_hidden.T.reshape(-1, tokens // BLOCK, BLOCK).transpose(1, 0, 2)
        pay = jnp.concatenate([teacher_hidden, stud.reshape(-1, BLOCK)], axis=0)
        pay = lax.ppermute(pay, ("x", "y"), spread_out)
        open_ = (allowed > 0).T.astype(jnp.float32)
        before = jnp.triu(jnp.ones((tokens, tokens), jnp.float32), 1)
        place = dot(open_.astype(jnp.bfloat16), before.astype(jnp.bfloat16), ((1,), (0,)))
        own_pos = jnp.where(open_ > 0, place.astype(jnp.int32), -1)
        own_pos = jnp.pad(own_pos, ((0, -blocks % 8), (0, 0)), constant_values=-1)
        places = [to_owner(own_pos, step) for step in range(sx)]
        most = functools.reduce(jnp.maximum, [jnp.max(p) for p in places])
        flag = jnp.full((1, 128), most, jnp.int32)
        flags = lax.all_to_all(
            jnp.broadcast_to(flag[None], (sx * sz * sc, 1, 128)), LOCAL, 0, 0, tiled=True
        )
        fits = jnp.max(flags) < CAP
        pay = lax.all_gather(pay, "z") if sz > 1 else pay[None]
        place_of = (lax.axis_index("y") * sz + lax.axis_index("z")) * sc + lax.axis_index("c")
        target = sampled - place_of * width
        return lax.cond(
            fits, compact, dense, pay, head_t, head_s, allowed, target, places, own_pos
        )

    return per_device


def solution(mesh, sizes=(4, 8, 2)):
    sx, sz, sc = sizes
    grid = Mesh(mesh.devices.reshape(sx, sx, sz, sc), ("x", "y", "z", "c"))
    both = P("x", LOCAL)
    return jax.shard_map(
        build(sx, sz, sc),
        mesh=grid,
        in_specs=(both, both, both, both, both, P("x")),
        out_specs=(P("x"), P("x"), both),
        check_vma=False,
    )
```

```python
import functools

import jax
import jax.numpy as jnp
from jax import lax
from jax.experimental import pallas as pl
from jax.experimental.pallas import tpu as pltpu
from jax.sharding import Mesh
from jax.sharding import PartitionSpec as P

CAP = 80
NEG = -1e30
BLOCK = 128
LOCAL = ("y", "z", "c")


def dot(a, b, dims):
    return lax.dot_general(a, b, (dims, ((), ())), preferred_element_type=jnp.float32)


def params(**kw):
    return pltpu.CompilerParams(vmem_limit_bytes=48 << 20, **kw)


def selector(pos_row):
    lines = lax.broadcasted_iota(jnp.int32, (CAP, pos_row.shape[-1]), 0)
    return lines == pos_row


def partial_kernel(core, pos, *refs):
    count = pos.shape[0]
    mine, others = refs[:count], refs[count : 2 * count]
    head_t, head_s, out, kept, sel, rows_t, rows_s = refs[2 * count :]
    blocks = sel.shape[0] // CAP
    depth, tokens = mine[0].shape[0], sel.shape[1]
    both = kept.shape[1] // depth
    b = pl.program_id(0)

    @pl.when(b == 0)
    def _():
        first = core[0] == 0
        for i in range(count):
            for k in range(blocks):
                mark = selector(pos[i, k : k + 1, :]).astype(jnp.float32)
                sel[k * CAP : (k + 1) * CAP, :] = mark.astype(jnp.bfloat16)

            def chunk(z, _, i=i):
                a, o = mine[i][z, :tokens, :], others[i][z, :tokens, :]
                pair = jnp.concatenate([jnp.where(first, a, o), jnp.where(first, o, a)], axis=1)
                rows_t[i, :, pl.ds(pl.multiple_of(z * 256, 256), 256)] = dot(
                    sel[...], pair, ((1,), (0,))
                ).astype(jnp.bfloat16)
                a = mine[i][z, tokens:, :].astype(jnp.float32)
                o = others[i][z, tokens:, :].astype(jnp.float32)
                parts = []
                for part in (jnp.where(first, a, o), jnp.where(first, o, a)):
                    parts.append(jnp.concatenate([part[: both // 2], part[both // 2 :]], axis=1))
                kept[i, pl.ds(pl.multiple_of(z * both, 16), both), :] = jnp.concatenate(
                    parts, axis=0
                ).astype(jnp.bfloat16)
                return 0

            lax.fori_loop(0, depth, chunk, 0)
            deep_s = kept.shape[1]
            for at in range(0, deep_s, 256):
                end = min(at + 256, deep_s)
                rows_s[i, :, at:end] = dot(sel[...], kept[i, at:end, :], ((1,), (1,))).astype(
                    jnp.bfloat16
                )

    here = pl.ds(pl.multiple_of(b * CAP, 16), CAP)
    deep_t, deep_s = rows_t.shape[-1], rows_s.shape[-1]
    out[:, 0, 0] = dot(
        rows_t[:, here, :].reshape(count * CAP, deep_t), head_t[...], ((1,), (0,))
    ).reshape(count, CAP, BLOCK)
    out[:, 1, 0] = dot(
        rows_s[:, here, :].reshape(count * CAP, deep_s), head_s[...], ((1,), (0,))
    ).reshape(count, CAP, BLOCK)


def partial_logits(core, pos, mine, others, head_t, head_s, tokens):
    count = len(mine)
    deep_t, width = head_t.shape
    deep_s = head_s.shape[0]
    blocks = width // BLOCK
    whole = lambda a: pl.BlockSpec(a.shape, lambda b, core: (0,) * a.ndim)
    return pl.pallas_call(
        partial_kernel,
        name="partial_logits",
        grid_spec=pltpu.PrefetchScalarGridSpec(
            num_scalar_prefetch=1,
            grid=(blocks,),
            in_specs=[whole(pos)]
            + [whole(a) for a in (*mine, *others)]
            + [
                pl.BlockSpec((deep_t, BLOCK), lambda b, core: (0, b)),
                pl.BlockSpec((deep_s, BLOCK), lambda b, core: (0, b)),
            ],
            out_specs=[
                pl.BlockSpec((count, 2, 1, CAP, BLOCK), lambda b, core: (0, 0, b, 0, 0)),
                pl.BlockSpec((count, deep_s, tokens), lambda b, core: (0, 0, 0)),
            ],
            scratch_shapes=[
                pltpu.VMEM((blocks * CAP, tokens), jnp.bfloat16),
                pltpu.VMEM((count, blocks * CAP, deep_t), jnp.bfloat16),
                pltpu.VMEM((count, blocks * CAP, deep_s), jnp.bfloat16),
            ],
        ),
        out_shape=[
            jax.ShapeDtypeStruct((count, 2, blocks, CAP, BLOCK), jnp.float32),
            jax.ShapeDtypeStruct((count, deep_s, tokens), jnp.bfloat16),
        ],
        compiler_params=params(),
        cost_estimate=pl.CostEstimate(
            flops=8 * count * blocks * CAP * (deep_t + deep_s) * tokens,
            bytes_accessed=2 * (deep_t + deep_s) * (width + count * tokens),
            transcendentals=0,
        ),
    )(core, pos, *mine, *others, head_t, head_s)


def spread(mark, line):
    return jnp.sum(jnp.where(mark, line, jnp.zeros_like(line)), axis=1, keepdims=True)


def fold(mark, column):
    return jnp.sum(jnp.where(mark, column, jnp.zeros_like(column)), axis=0, keepdims=True)


def stats_kernel(pos, target, places, a0, a1, a2, a3, logits, stats):
    blocks = logits.shape[1]
    tokens = pos.shape[-1]
    tops = [jnp.full((1, tokens), NEG, jnp.float32) for _ in range(2)]
    for b in range(blocks):
        mark = selector(pos[b : b + 1, :])
        for h in range(2):
            total = (a0[0, h, b] + a1[0, h, b]) + (a2[0, h, b] + a3[0, h, b])
            logits[h, b] = total
            peak = jnp.max(total, axis=1, keepdims=True)
            tops[h] = jnp.maximum(
                tops[h], jnp.max(jnp.where(mark, peak, NEG), axis=0, keepdims=True)
            )
    zero = jnp.zeros((1, tokens), jnp.float32)
    sum_t, cross, sum_s, picked = zero, zero, zero, zero
    lanes = lax.broadcasted_iota(jnp.int32, (CAP, BLOCK), 1)
    for b in range(blocks):
        mark = selector(pos[b : b + 1, :])
        lt, ls = logits[0, b], logits[1, b]
        et = jnp.exp(lt - spread(mark, tops[0]))
        es = jnp.exp(ls - spread(mark, tops[1]))
        wanted = spread(mark, target[...] - b * BLOCK)
        sum_t = sum_t + fold(mark, jnp.sum(et, axis=1, keepdims=True))
        cross = cross + fold(mark, jnp.sum(et * (lt - ls), axis=1, keepdims=True))
        sum_s = sum_s + fold(mark, jnp.sum(es, axis=1, keepdims=True))
        picked = picked + fold(
            mark, jnp.sum(jnp.where(lanes == wanted, ls, 0.0), axis=1, keepdims=True)
        )
    most = jnp.max(places[...].astype(jnp.float32), axis=(0, 1))[None]
    most = jnp.broadcast_to(jnp.max(most, axis=1, keepdims=True), zero.shape)
    lines = [tops[0], sum_t, cross, tops[1], sum_s, picked, most, zero]
    stats[...] = jnp.concatenate(lines, axis=0)


def row_stats(pos, target, places, parts):
    blocks = parts[0].shape[2]
    return pl.pallas_call(
        stats_kernel,
        name="row_stats",
        out_shape=[
            jax.ShapeDtypeStruct((2, blocks, CAP, BLOCK), jnp.float32),
            jax.ShapeDtypeStruct((8, pos.shape[-1]), jnp.float32),
        ],
        compiler_params=params(),
    )(pos, target, places, *parts)


def combined(seen):
    top_t = jnp.max(seen[:, 0, :], axis=0, keepdims=True)
    top_s = jnp.max(seen[:, 3, :], axis=0, keepdims=True)
    scale_t = jnp.exp(seen[:, 0, :] - top_t)
    scale_s = jnp.exp(seen[:, 3, :] - top_s)
    total = lambda a: jnp.sum(a, axis=0, keepdims=True)
    sum_t = total(seen[:, 1, :] * scale_t)
    cross = total(seen[:, 2, :] * scale_t)
    sum_s = total(seen[:, 4, :] * scale_s)
    picked = total(seen[:, 5, :])
    log_t = top_t + jnp.log(sum_t)
    log_s = top_s + jnp.log(sum_s)
    return top_t, sum_t, top_s, sum_s, cross / sum_t - log_t + log_s, picked - log_s


def grad_kernel(pos, seen, logits, grad, rows):
    top_t, sum_t, top_s, sum_s, row_kl, logprob = combined(seen[...])
    most = jnp.max(seen[:, 6, :], axis=0, keepdims=True)
    rows[...] = jnp.concatenate([row_kl, logprob, most] + [most] * 5, axis=0)
    inv_t, inv_s = 1.0 / sum_t, 1.0 / sum_s
    for b in range(logits.shape[1]):
        mark = selector(pos[b : b + 1, :])
        et = jnp.exp(logits[0, b] - spread(mark, top_t)) * spread(mark, inv_t)
        es = jnp.exp(logits[1, b] - spread(mark, top_s)) * spread(mark, inv_s)
        grad[b] = (es - et).astype(jnp.bfloat16)


def row_grads(pos, seen, logits):
    return pl.pallas_call(
        grad_kernel,
        name="row_grads",
        out_shape=[
            jax.ShapeDtypeStruct(logits.shape[1:], jnp.bfloat16),
            jax.ShapeDtypeStruct((8, pos.shape[-1]), jnp.float32),
        ],
        compiler_params=params(),
    )(pos, seen, logits)


def head_kernel(places, *refs):
    *studs, out, left = refs
    grads, studs = studs[:4], studs[4:]
    tokens = places.shape[-1]
    b = pl.program_id(0)

    @pl.when(b == 0)
    def _():
        at = 0
        for ref in studs:
            for i in range(ref.shape[0]):
                left[:, at : at + tokens] = ref[i]
                at += tokens

    right = []
    for t, grad in enumerate(grads):
        pair = []
        for k in range(2):
            mark = selector(places[t, 2 * b + k][None]).astype(jnp.float32).astype(jnp.bfloat16)
            pair.append(dot(mark, grad[k], ((0,), (0,))).astype(jnp.bfloat16))
        right.append(jnp.concatenate(pair, axis=1))
    out[...] = dot(left[...], jnp.concatenate(right, axis=0), ((1,), (0,)))


def head_gradient(places, grads, studs):
    deep, tokens = studs[0].shape[1:]
    blocks = grads[0].shape[0]
    whole = lambda a: pl.BlockSpec(a.shape, lambda b: (0,) * a.ndim)
    return pl.pallas_call(
        head_kernel,
        name="head_gradient",
        grid=(blocks // 2,),
        in_specs=[whole(places)]
        + [pl.BlockSpec((2, CAP, BLOCK), lambda b: (b, 0, 0)) for _ in grads]
        + [whole(a) for a in studs],
        out_specs=pl.BlockSpec((deep, 2 * BLOCK), lambda b: (0, b)),
        out_shape=jax.ShapeDtypeStruct((deep, blocks * BLOCK), jnp.float32),
        scratch_shapes=[pltpu.VMEM((deep, 4 * tokens), jnp.bfloat16)],
        compiler_params=params(),
    )(places, *grads, *studs)


def build(sx, sz, sc):
    turn = lambda step: [
        (x * sx + y, ((y + step - x) % sx) * sx + y) for x in range(sx) for y in range(sx)
    ]
    spread_out = [(x * sx + y, y * sx + (x + y) % sx) for x in range(sx) for y in range(sx)]
    shift = lambda step: [(y, (y + step) % sx) for y in range(sx)]

    def to_owner(a, step):
        return lax.ppermute(a, ("x", "y"), turn(step))

    def both_cores(mine):
        if sc == 1:
            return mine[:, None]
        other = lax.ppermute(mine, "c", [(0, 1), (1, 0)])
        first = lax.axis_index("c") == 0
        return jnp.stack([jnp.where(first, mine, other), jnp.where(first, other, mine)], axis=1)

    def features(pay, tokens):
        full = both_cores(pay)
        chunks = full.shape[0] * full.shape[1]
        full = full.reshape(chunks, -1, BLOCK)
        teach = full[:, :tokens]
        stud = full[:, tokens:].reshape(chunks, tokens // BLOCK, -1, BLOCK)
        stud = stud.transpose(0, 2, 1, 3).reshape(-1, tokens)
        return teach, stud

    def neighbours(pay):
        after = lax.ppermute(pay, "y", shift(-1))
        before = lax.ppermute(pay, "y", shift(1))
        return after, before

    def opposite(after, before):
        half = after.shape[0] // 2
        if half == 0:
            return lax.ppermute(after, "y", shift(-1))
        low = lax.ppermute(after[:half], "y", shift(-1))
        high = lax.ppermute(before[half:], "y", shift(1))
        return jnp.concatenate([low, high], axis=0)

    def everyone(stats):
        copies = jnp.broadcast_to(stats[None], (sx * sz * sc, *stats.shape))
        return lax.all_to_all(copies, LOCAL, split_axis=0, concat_axis=0, tiled=True)

    def dense(pays, head_t, head_s, allowed, target):
        tokens, blocks = allowed.shape
        width = head_t.shape[1]
        studs, total = {}, 0.0
        for step in range(sx):
            teach, stud = features(pays[step], tokens)
            studs[step] = stud
            teach = teach.transpose(1, 0, 2).reshape(tokens, -1)
            part = jnp.concatenate(
                [dot(teach, head_t, ((1,), (0,))), dot(stud, head_s, ((0,), (0,)))], axis=1
            )
            total = total + to_owner(part, step)
        lt, ls = total[:, :width], total[:, width:]
        open_ = jnp.broadcast_to((allowed > 0)[:, :, None], (tokens, blocks, BLOCK))
        open_ = open_.reshape(tokens, width)
        ids = jnp.arange(width, dtype=jnp.int32)
        picked = jnp.sum(jnp.where(ids[None, :] == target[:, None], ls, 0.0), axis=1)
        top_t = jnp.max(jnp.where(open_, lt, NEG), axis=1)
        top_s = jnp.max(jnp.where(open_, ls, NEG), axis=1)
        et = jnp.where(open_, jnp.exp(jnp.where(open_, lt, NEG) - top_t[:, None]), 0.0)
        es = jnp.where(open_, jnp.exp(jnp.where(open_, ls, NEG) - top_s[:, None]), 0.0)
        lines = [top_t, et.sum(1), (et * (lt - ls)).sum(1), top_s, es.sum(1), picked]
        stats = jnp.stack(lines + [jnp.zeros_like(top_t)] * 2)
        all_t, sum_t, all_s, sum_s, row_kl, logprob = combined(everyone(stats))
        scale_t = (jnp.exp(top_t[None] - all_t) / sum_t)[0]
        scale_s = (jnp.exp(top_s[None] - all_s) / sum_s)[0]
        grad = (es * scale_s[:, None] - et * scale_t[:, None]).astype(jnp.bfloat16)
        head = sum(
            dot(studs[step], to_owner(grad, step), ((1,), (0,))) for step in range(sx)
        )
        return row_kl[0], logprob[0], head

    def other_core(pay):
        return lax.ppermute(pay, "c", [(0, 1), (1, 0)]) if sc > 1 else pay

    def per_device(teacher_hidden, student_hidden, head_t, head_s, allowed, sampled):
        tokens, blocks = allowed.shape
        width = head_t.shape[1]
        stud = student_hidden.T.reshape(-1, tokens // BLOCK, BLOCK).transpose(1, 0, 2)
        pay = jnp.concatenate([teacher_hidden, stud.reshape(-1, BLOCK)], axis=0)
        pay = lax.ppermute(pay, ("x", "y"), spread_out)
        open_ = (allowed > 0).T.astype(jnp.float32)
        before = jnp.triu(jnp.ones((tokens, tokens), jnp.float32), 1)
        place = dot(open_.astype(jnp.bfloat16), before.astype(jnp.bfloat16), ((1,), (0,)))
        own_pos = jnp.where(open_ > 0, place.astype(jnp.int32), -1)
        own_pos = jnp.pad(own_pos, ((0, -blocks % 8), (0, 0)), constant_values=-1)
        order = (0, 1, 3, 2)
        places = jnp.stack([to_owner(own_pos, step) for step in order])
        pay = lax.all_to_all(
            jnp.broadcast_to(pay[None], (sz, *pay.shape)), "z", 0, 0, tiled=True
        )
        core = lax.axis_index("c").astype(jnp.int32)[None]
        place_of = (lax.axis_index("y") * sz + lax.axis_index("z")) * sc + lax.axis_index("c")
        target = sampled - place_of * width

        run = lambda at, mine, others: partial_logits(
            core, places[at], mine, others, head_t, head_s, tokens
        )
        pay, other = lax.optimization_barrier((pay, other_core(pay)))
        after, ahead = neighbours(pay)
        part, stud0 = run(slice(0, 1), [pay], [other])
        got = [to_owner(part, order[0])]
        far = opposite(after, ahead)
        part, stud1 = run(slice(1, 3), [after, ahead], [other_core(after), other_core(ahead)])
        got += [to_owner(part[:1], order[1]), to_owner(part[1:], order[2])]
        part, stud2 = run(slice(3, 4), [far], [other_core(far)])
        got.append(to_owner(part, order[3]))

        logits, stats = row_stats(own_pos, target[None], places, got)
        grad, rows = row_grads(own_pos, everyone(stats), logits)
        grads = [to_owner(grad, step) for step in order]
        head = head_gradient(places, grads, [stud0, stud1, stud2])
        start = (rows[2, 0] >= CAP, rows[0], rows[1], head)
        pays = {0: pay, 1: after, 3: ahead, 2: far}

        def redo(_):
            return (False, *dense(pays, head_t, head_s, allowed, target))

        return lax.while_loop(lambda held: held[0], redo, start)[1:]

    return per_device


def solution(mesh, sizes=(4, 8, 2)):
    sx, sz, sc = sizes
    grid = Mesh(mesh.devices.reshape(sx, sx, sz, sc), ("x", "y", "z", "c"))
    both = P("x", LOCAL)
    return jax.shard_map(
        build(sx, sz, sc),
        mesh=grid,
        in_specs=(both, both, both, both, both, P("x")),
        out_specs=(P("x"), P("x"), both),
        check_vma=False,
    )
```

```python
import functools

import jax
import jax.numpy as jnp
from jax import lax
from jax.experimental import pallas as pl
from jax.experimental.pallas import tpu as pltpu
from jax.sharding import Mesh
from jax.sharding import PartitionSpec as P

CAP = 80
NEG = -1e30
BLOCK = 128
LOCAL = ("y", "z", "c")


def dot(a, b, dims):
    return lax.dot_general(a, b, (dims, ((), ())), preferred_element_type=jnp.float32)


def params(**kw):
    return pltpu.CompilerParams(vmem_limit_bytes=48 << 20, **kw)


def selector(pos_row):
    lines = lax.broadcasted_iota(jnp.int32, (CAP, pos_row.shape[-1]), 0)
    return lines == pos_row


def diagonal():
    rows = lax.broadcasted_iota(jnp.int32, (CAP, BLOCK), 0)
    return rows == lax.broadcasted_iota(jnp.int32, (CAP, BLOCK), 1)


def coded(logits):
    peak = jnp.max(jnp.abs(logits), axis=1, keepdims=True)
    power = jnp.floor(jnp.log2(jnp.maximum(peak, 1e-30)))
    scaled = jnp.round(logits * jnp.exp2(14.0 - power))
    values = jnp.clip(scaled, -32767.0, 32767.0).astype(jnp.int32).astype(jnp.int16)
    return values, jnp.sum(jnp.where(diagonal(), power, 0.0), axis=0, keepdims=True)


def decoded(values, powers):
    power = jnp.sum(jnp.where(diagonal(), powers, 0.0), axis=1, keepdims=True)
    return values.astype(jnp.int32).astype(jnp.float32) * jnp.exp2(power - 14.0)


def partial_kernel(steps, meta, pos, *refs):
    count = len(steps)
    mine, others = refs[:count], refs[count : 2 * count]
    head_t, head_s = refs[2 * count : 2 * count + 2]
    outs = refs[2 * count + 2 : 3 * count + 2]
    kept, sel, rows_t, rows_s, powers = refs[3 * count + 2 :]
    blocks = sel.shape[0] // CAP
    depth, tokens = mine[0].shape[0], sel.shape[1]
    both = kept.shape[1] // depth
    b = pl.program_id(0)

    @pl.when(b == 0)
    def _():
        first = meta[0] == 0
        powers[...] = jnp.zeros_like(powers)
        for i in range(count):
            held = meta[1 + steps[i]]
            for k in range(blocks):
                mark = selector(pos[held, k : k + 1, :]).astype(jnp.float32)
                sel[k * CAP : (k + 1) * CAP, :] = mark.astype(jnp.bfloat16)

            def chunk(z, _, i=i):
                a, o = mine[i][z, :tokens, :], others[i][z, :tokens, :]
                pair = jnp.concatenate([jnp.where(first, a, o), jnp.where(first, o, a)], axis=1)
                rows_t[i, :, pl.ds(pl.multiple_of(z * 256, 256), 256)] = dot(
                    sel[...], pair, ((1,), (0,))
                ).astype(jnp.bfloat16)
                a = mine[i][z, tokens:, :].astype(jnp.float32)
                o = others[i][z, tokens:, :].astype(jnp.float32)
                parts = []
                for part in (jnp.where(first, a, o), jnp.where(first, o, a)):
                    parts.append(jnp.concatenate([part[: both // 2], part[both // 2 :]], axis=1))
                kept[i, pl.ds(pl.multiple_of(z * both, 16), both), :] = jnp.concatenate(
                    parts, axis=0
                ).astype(jnp.bfloat16)
                return 0

            lax.fori_loop(0, depth, chunk, 0)
            deep_s = kept.shape[1]
            for at in range(0, deep_s, 256):
                end = min(at + 256, deep_s)
                rows_s[i, :, at:end] = dot(sel[...], kept[i, at:end, :], ((1,), (1,))).astype(
                    jnp.bfloat16
                )

    here = pl.ds(pl.multiple_of(b * 2 * CAP, 16), 2 * CAP)
    for h, (rows, head) in enumerate(((rows_t, head_t), (rows_s, head_s))):
        lines = rows[:, here, :].reshape(count * 2 * CAP, rows.shape[-1])
        product = dot(lines, head[...], ((1,), (0,)))
        for i in range(count):
            for k in range(2):
                at = (2 * i + k) * CAP
                values, power = coded(product[at : at + CAP, k * BLOCK : (k + 1) * BLOCK])
                outs[i][0, h, pl.ds(pl.multiple_of((2 * b + k) * CAP, 16), CAP), :] = values
                powers[2 * i + h, pl.ds(2 * b + k, 1), :] = power

    @pl.when(b == pl.num_programs(0) - 1)
    def _():
        for i in range(count):
            for h in range(2):
                outs[i][0, h, blocks * CAP :, :] = (
                    powers[2 * i + h].astype(jnp.int32).astype(jnp.int16)
                )


def partial_logits(meta, pos, steps, mine, others, head_t, head_s):
    count = len(steps)
    tokens = pos.shape[-1]
    deep_t, width = head_t.shape
    deep_s = head_s.shape[0]
    blocks = width // BLOCK
    coded_rows = blocks * CAP + 16
    whole = lambda a: pl.BlockSpec(a.shape, lambda b, meta: (0,) * a.ndim)
    return pl.pallas_call(
        functools.partial(partial_kernel, steps),
        name="partial_logits",
        grid_spec=pltpu.PrefetchScalarGridSpec(
            num_scalar_prefetch=1,
            grid=(blocks // 2,),
            in_specs=[whole(pos)]
            + [whole(a) for a in (*mine, *others)]
            + [
                pl.BlockSpec((deep_t, 2 * BLOCK), lambda b, meta: (0, b)),
                pl.BlockSpec((deep_s, 2 * BLOCK), lambda b, meta: (0, b)),
            ],
            out_specs=[pl.BlockSpec((1, 2, coded_rows, BLOCK), lambda b, meta: (0, 0, 0, 0))] * count
            + [pl.BlockSpec((count, deep_s, tokens), lambda b, meta: (0, 0, 0))],
            scratch_shapes=[
                pltpu.VMEM((blocks * CAP, tokens), jnp.bfloat16),
                pltpu.VMEM((count, blocks * CAP, deep_t), jnp.bfloat16),
                pltpu.VMEM((count, blocks * CAP, deep_s), jnp.bfloat16),
                pltpu.VMEM((2 * count, 16, BLOCK), jnp.float32),
            ],
        ),
        out_shape=[jax.ShapeDtypeStruct((1, 2, coded_rows, BLOCK), jnp.int16)] * count
        + [jax.ShapeDtypeStruct((count, deep_s, tokens), jnp.bfloat16)],
        compiler_params=params(),
        cost_estimate=pl.CostEstimate(
            flops=8 * count * blocks * CAP * (deep_t + deep_s) * tokens,
            bytes_accessed=2 * (deep_t + deep_s) * (width + count * tokens),
            transcendentals=0,
        ),
    )(meta, pos, *mine, *others, head_t, head_s)


def spread(mark, line):
    return jnp.sum(jnp.where(mark, line, jnp.zeros_like(line)), axis=1, keepdims=True)


def fold(mark, column):
    return jnp.sum(jnp.where(mark, column, jnp.zeros_like(column)), axis=0, keepdims=True)


def stats_kernel(pos, target, places, a0, a1, a2, a3, logits, stats):
    blocks = logits.shape[1]
    tokens = pos.shape[-1]
    tops = [jnp.full((1, tokens), NEG, jnp.float32) for _ in range(2)]
    first = blocks * CAP
    powers = [
        [a[0, h, first:, :].astype(jnp.int32).astype(jnp.float32) for a in (a0, a1, a2, a3)]
        for h in range(2)
    ]
    for b in range(blocks):
        mark = selector(pos[b : b + 1, :])
        for h in range(2):
            total = 0.0
            for a, power in zip((a0, a1, a2, a3), powers[h]):
                total = total + decoded(a[0, h, b * CAP : (b + 1) * CAP, :], power[b : b + 1, :])
            logits[h, b] = total
            peak = jnp.max(total, axis=1, keepdims=True)
            tops[h] = jnp.maximum(
                tops[h], jnp.max(jnp.where(mark, peak, NEG), axis=0, keepdims=True)
            )
    zero = jnp.zeros((1, tokens), jnp.float32)
    sum_t, cross, sum_s, picked = zero, zero, zero, zero
    lanes = lax.broadcasted_iota(jnp.int32, (CAP, BLOCK), 1)
    for b in range(blocks):
        mark = selector(pos[b : b + 1, :])
        lt, ls = logits[0, b], logits[1, b]
        et = jnp.exp(lt - spread(mark, tops[0]))
        es = jnp.exp(ls - spread(mark, tops[1]))
        wanted = spread(mark, target[...] - b * BLOCK)
        sum_t = sum_t + fold(mark, jnp.sum(et, axis=1, keepdims=True))
        cross = cross + fold(mark, jnp.sum(et * (lt - ls), axis=1, keepdims=True))
        sum_s = sum_s + fold(mark, jnp.sum(es, axis=1, keepdims=True))
        picked = picked + fold(
            mark, jnp.sum(jnp.where(lanes == wanted, ls, 0.0), axis=1, keepdims=True)
        )
    most = jnp.max(places[...].astype(jnp.float32), axis=(0, 1))[None]
    most = jnp.broadcast_to(jnp.max(most, axis=1, keepdims=True), zero.shape)
    lines = [tops[0], sum_t, cross, tops[1], sum_s, picked, most, zero]
    stats[...] = jnp.concatenate(lines, axis=0)


def row_stats(pos, target, places, parts):
    blocks = parts[0].shape[2] // CAP
    return pl.pallas_call(
        stats_kernel,
        name="row_stats",
        out_shape=[
            jax.ShapeDtypeStruct((2, blocks, CAP, BLOCK), jnp.float32),
            jax.ShapeDtypeStruct((8, pos.shape[-1]), jnp.float32),
        ],
        compiler_params=params(),
    )(pos, target, places, *parts)


def combined(seen):
    top_t = jnp.max(seen[:, 0, :], axis=0, keepdims=True)
    top_s = jnp.max(seen[:, 3, :], axis=0, keepdims=True)
    scale_t = jnp.exp(seen[:, 0, :] - top_t)
    scale_s = jnp.exp(seen[:, 3, :] - top_s)
    total = lambda a: jnp.sum(a, axis=0, keepdims=True)
    sum_t = total(seen[:, 1, :] * scale_t)
    cross = total(seen[:, 2, :] * scale_t)
    sum_s = total(seen[:, 4, :] * scale_s)
    picked = total(seen[:, 5, :])
    log_t = top_t + jnp.log(sum_t)
    log_s = top_s + jnp.log(sum_s)
    return top_t, sum_t, top_s, sum_s, cross / sum_t - log_t + log_s, picked - log_s


def grad_kernel(pos, seen, logits, grad, rows):
    top_t, sum_t, top_s, sum_s, row_kl, logprob = combined(seen[...])
    most = jnp.max(seen[:, 6, :], axis=0, keepdims=True)
    rows[...] = jnp.concatenate([row_kl, logprob, most] + [most] * 5, axis=0)
    inv_t, inv_s = 1.0 / sum_t, 1.0 / sum_s
    for b in range(logits.shape[1]):
        mark = selector(pos[b : b + 1, :])
        et = jnp.exp(logits[0, b] - spread(mark, top_t)) * spread(mark, inv_t)
        es = jnp.exp(logits[1, b] - spread(mark, top_s)) * spread(mark, inv_s)
        grad[b] = (es - et).astype(jnp.bfloat16)


def row_grads(pos, seen, logits):
    return pl.pallas_call(
        grad_kernel,
        name="row_grads",
        out_shape=[
            jax.ShapeDtypeStruct(logits.shape[1:], jnp.bfloat16),
            jax.ShapeDtypeStruct((8, pos.shape[-1]), jnp.float32),
        ],
        compiler_params=params(),
    )(pos, seen, logits)


def head_kernel(meta, places, *refs):
    *studs, out, left = refs
    grads, studs = studs[:4], studs[4:]
    tokens = places.shape[-1]
    b = pl.program_id(0)

    @pl.when(b == 0)
    def _():
        step = 1
        for ref in studs:
            for i in range(ref.shape[0]):
                at = pl.multiple_of(meta[step] * tokens, tokens)
                left[:, pl.ds(at, tokens)] = ref[i]
                step += 1

    right = []
    for t, grad in enumerate(grads):
        pair = []
        for k in range(2):
            mark = selector(places[t, 2 * b + k][None]).astype(jnp.float32).astype(jnp.bfloat16)
            pair.append(dot(mark, grad[k], ((0,), (0,))).astype(jnp.bfloat16))
        right.append(jnp.concatenate(pair, axis=1))
    out[...] = dot(left[...], jnp.concatenate(right, axis=0), ((1,), (0,)))


def head_gradient(meta, places, grads, studs):
    deep, tokens = studs[0].shape[1:]
    blocks = grads[0].shape[0]
    whole = lambda a: pl.BlockSpec(a.shape, lambda b, meta: (0,) * a.ndim)
    return pl.pallas_call(
        head_kernel,
        name="head_gradient",
        grid_spec=pltpu.PrefetchScalarGridSpec(
            num_scalar_prefetch=1,
            grid=(blocks // 2,),
            in_specs=[whole(places)]
            + [pl.BlockSpec((2, CAP, BLOCK), lambda b, meta: (b, 0, 0)) for _ in grads]
            + [whole(a) for a in studs],
            out_specs=pl.BlockSpec((deep, 2 * BLOCK), lambda b, meta: (0, b)),
            scratch_shapes=[pltpu.VMEM((deep, 4 * tokens), jnp.bfloat16)],
        ),
        out_shape=jax.ShapeDtypeStruct((deep, blocks * BLOCK), jnp.float32),
        compiler_params=params(),
    )(meta, places, *grads, *studs)


def build(sx, sz, sc):
    turn = lambda step: [
        (x * sx + y, ((y + step - x) % sx) * sx + y) for x in range(sx) for y in range(sx)
    ]
    spread_out = [(x * sx + y, y * sx + (x + y) % sx) for x in range(sx) for y in range(sx)]
    shift = lambda step: [(y, (y + step) % sx) for y in range(sx)]

    def to_owner(a, step):
        return lax.ppermute(a, ("x", "y"), turn(step))

    def both_cores(mine):
        if sc == 1:
            return mine[:, None]
        other = lax.ppermute(mine, "c", [(0, 1), (1, 0)])
        first = lax.axis_index("c") == 0
        return jnp.stack([jnp.where(first, mine, other), jnp.where(first, other, mine)], axis=1)

    def features(pay, tokens):
        full = both_cores(pay)
        chunks = full.shape[0] * full.shape[1]
        full = full.reshape(chunks, -1, BLOCK)
        teach = full[:, :tokens]
        stud = full[:, tokens:].reshape(chunks, tokens // BLOCK, -1, BLOCK)
        stud = stud.transpose(0, 2, 1, 3).reshape(-1, tokens)
        return teach, stud

    def neighbours(pay):
        after = lax.ppermute(pay, "y", shift(-1))
        before = lax.ppermute(pay, "y", shift(1))
        return after, before

    def opposite(after, before):
        half = after.shape[0] // 2
        if half == 0:
            return lax.ppermute(after, "y", shift(-1))
        low = lax.ppermute(after[:half], "y", shift(-1))
        high = lax.ppermute(before[half:], "y", shift(1))
        return jnp.concatenate([low, high], axis=0)

    def everyone(stats):
        copies = jnp.broadcast_to(stats[None], (sx * sz * sc, *stats.shape))
        return lax.all_to_all(copies, LOCAL, split_axis=0, concat_axis=0, tiled=True)

    def dense(pays, head_t, head_s, allowed, target):
        tokens, blocks = allowed.shape
        width = head_t.shape[1]
        studs, total = {}, 0.0
        for step in range(sx):
            teach, stud = features(pays[step], tokens)
            studs[step] = stud
            teach = teach.transpose(1, 0, 2).reshape(tokens, -1)
            part = jnp.concatenate(
                [dot(teach, head_t, ((1,), (0,))), dot(stud, head_s, ((0,), (0,)))], axis=1
            )
            total = total + to_owner(part, step)
        lt, ls = total[:, :width], total[:, width:]
        open_ = jnp.broadcast_to((allowed > 0)[:, :, None], (tokens, blocks, BLOCK))
        open_ = open_.reshape(tokens, width)
        ids = jnp.arange(width, dtype=jnp.int32)
        picked = jnp.sum(jnp.where(ids[None, :] == target[:, None], ls, 0.0), axis=1)
        top_t = jnp.max(jnp.where(open_, lt, NEG), axis=1)
        top_s = jnp.max(jnp.where(open_, ls, NEG), axis=1)
        et = jnp.where(open_, jnp.exp(jnp.where(open_, lt, NEG) - top_t[:, None]), 0.0)
        es = jnp.where(open_, jnp.exp(jnp.where(open_, ls, NEG) - top_s[:, None]), 0.0)
        lines = [top_t, et.sum(1), (et * (lt - ls)).sum(1), top_s, es.sum(1), picked]
        stats = jnp.stack(lines + [jnp.zeros_like(top_t)] * 2)
        all_t, sum_t, all_s, sum_s, row_kl, logprob = combined(everyone(stats))
        scale_t = (jnp.exp(top_t[None] - all_t) / sum_t)[0]
        scale_s = (jnp.exp(top_s[None] - all_s) / sum_s)[0]
        grad = (es * scale_s[:, None] - et * scale_t[:, None]).astype(jnp.bfloat16)
        head = sum(
            dot(studs[step], to_owner(grad, step), ((1,), (0,))) for step in range(sx)
        )
        return row_kl[0], logprob[0], head

    def other_core(pay):
        return lax.ppermute(pay, "c", [(0, 1), (1, 0)]) if sc > 1 else pay

    def per_device(teacher_hidden, student_hidden, head_t, head_s, allowed, sampled):
        tokens, blocks = allowed.shape
        width = head_t.shape[1]
        stud = student_hidden.T.reshape(-1, tokens // BLOCK, BLOCK).transpose(1, 0, 2)
        pay = jnp.concatenate([teacher_hidden, stud.reshape(-1, BLOCK)], axis=0)
        pay = lax.ppermute(pay, ("x", "y"), spread_out)
        open_ = (allowed > 0).T.astype(jnp.float32)
        before = jnp.triu(jnp.ones((tokens, tokens), jnp.float32), 1)
        place = dot(open_.astype(jnp.bfloat16), before.astype(jnp.bfloat16), ((1,), (0,)))
        own_pos = jnp.where(open_ > 0, place.astype(jnp.int32), -1)
        own_pos = jnp.pad(own_pos, ((0, -blocks % 8), (0, 0)), constant_values=-1)
        order = (0, 1, 3, 2)
        from_line = lambda a, far: lax.ppermute(a, "x", [(x, (x - far) % sx) for x in range(sx)])
        places = [own_pos] + [from_line(own_pos, far) for far in range(1, sx)]
        pay, places = lax.optimization_barrier((pay, places))
        places = jnp.stack(places)
        pay = lax.all_to_all(
            jnp.broadcast_to(pay[None], (sz, *pay.shape)), "z", 0, 0, tiled=True
        )
        here, row, core = (lax.axis_index(name).astype(jnp.int32) for name in ("x", "y", "c"))
        meta = jnp.stack([core] + [(row + step - 2 * here) % sx for step in order])
        place_of = (row * sz + lax.axis_index("z")) * sc + core
        target = sampled - place_of * width

        def run(steps, mine, others):
            return partial_logits(meta, places, steps, mine, others, head_t, head_s)

        pay, other = lax.optimization_barrier((pay, other_core(pay)))
        after, ahead = neighbours(pay)
        part, stud0 = run((0,), [pay], [other])
        got = [to_owner(part, order[0])]
        far = opposite(after, ahead)
        part, other_part, stud1 = run((1, 2), [after, ahead], [other_core(after), other_core(ahead)])
        got += [to_owner(part, order[1]), to_owner(other_part, order[2])]
        part, stud2 = run((3,), [far], [other_core(far)])
        got.append(to_owner(part, order[3]))

        logits, stats = row_stats(own_pos, target[None], places, got)
        grad, rows = row_grads(own_pos, everyone(stats), logits)
        grads = [grad] + [from_line(grad, far) for far in range(1, sx)]
        head = head_gradient(meta, places, grads, [stud0, stud1, stud2])
        start = (rows[2, 0] >= CAP, rows[0], rows[1], head)
        pays = {0: pay, 1: after, 3: ahead, 2: far}

        def redo(_):
            return (False, *dense(pays, head_t, head_s, allowed, target))

        return lax.while_loop(lambda held: held[0], redo, start)[1:]

    return per_device


def solution(mesh, sizes=(4, 8, 2)):
    sx, sz, sc = sizes
    grid = Mesh(mesh.devices.reshape(sx, sx, sz, sc), ("x", "y", "z", "c"))
    both = P("x", LOCAL)
    return jax.shard_map(
        build(sx, sz, sc),
        mesh=grid,
        in_specs=(both, both, both, both, both, P("x")),
        out_specs=(P("x"), P("x"), both),
        check_vma=False,
    )
```

```python
import functools

import jax
import jax.numpy as jnp
from jax import lax
from jax.experimental import pallas as pl
from jax.experimental.pallas import tpu as pltpu
from jax.sharding import Mesh
from jax.sharding import PartitionSpec as P

CAP = 80
NEG = -1e30
BLOCK = 128
LOCAL = ("y", "z", "c")


def dot(a, b, dims):
    return lax.dot_general(a, b, (dims, ((), ())), preferred_element_type=jnp.float32)


def params(**kw):
    return pltpu.CompilerParams(vmem_limit_bytes=48 << 20, **kw)


def selector(pos_row):
    lines = lax.broadcasted_iota(jnp.int32, (CAP, pos_row.shape[-1]), 0)
    return lines == pos_row


def diagonal():
    rows = lax.broadcasted_iota(jnp.int32, (CAP, BLOCK), 0)
    return rows == lax.broadcasted_iota(jnp.int32, (CAP, BLOCK), 1)


def coded(logits):
    peak = jnp.max(jnp.abs(logits), axis=1, keepdims=True)
    power = jnp.floor(jnp.log2(jnp.maximum(peak, 1e-30)))
    scaled = jnp.round(logits * jnp.exp2(14.0 - power))
    values = jnp.clip(scaled, -32767.0, 32767.0).astype(jnp.int32).astype(jnp.int16)
    return values, jnp.sum(jnp.where(diagonal(), power, 0.0), axis=0, keepdims=True)


def decoded(values, powers):
    power = jnp.sum(jnp.where(diagonal(), powers, 0.0), axis=1, keepdims=True)
    return values.astype(jnp.int32).astype(jnp.float32) * jnp.exp2(power - 14.0)


def partial_kernel(steps, meta, pos, *refs):
    count = len(steps)
    mine, others = refs[:count], refs[count : 2 * count]
    head_t, head_s = refs[2 * count : 2 * count + 2]
    outs = refs[2 * count + 2 : 3 * count + 2]
    kept, sel, rows_t, rows_s, powers = refs[3 * count + 2 :]
    blocks = sel.shape[0] // CAP
    depth, tokens = mine[0].shape[0], sel.shape[1]
    both = kept.shape[1] // depth
    b = pl.program_id(0)

    @pl.when(b == 0)
    def _():
        first = meta[0] == 0
        powers[...] = jnp.zeros_like(powers)
        for i in range(count):
            held = meta[1 + steps[i]]
            for k in range(blocks):
                mark = selector(pos[held, k : k + 1, :]).astype(jnp.float32)
                sel[k * CAP : (k + 1) * CAP, :] = mark.astype(jnp.bfloat16)

            def chunk(z, _, i=i):
                a, o = mine[i][z, :tokens, :], others[i][z, :tokens, :]
                pair = jnp.concatenate([jnp.where(first, a, o), jnp.where(first, o, a)], axis=1)
                rows_t[i, :, pl.ds(pl.multiple_of(z * 256, 256), 256)] = dot(
                    sel[...], pair, ((1,), (0,))
                ).astype(jnp.bfloat16)
                a = mine[i][z, tokens:, :].astype(jnp.float32)
                o = others[i][z, tokens:, :].astype(jnp.float32)
                parts = []
                for part in (jnp.where(first, a, o), jnp.where(first, o, a)):
                    parts.append(jnp.concatenate([part[: both // 2], part[both // 2 :]], axis=1))
                kept[i, pl.ds(pl.multiple_of(z * both, 16), both), :] = jnp.concatenate(
                    parts, axis=0
                ).astype(jnp.bfloat16)
                return 0

            lax.fori_loop(0, depth, chunk, 0)
            deep_s = kept.shape[1]
            for at in range(0, deep_s, 256):
                end = min(at + 256, deep_s)
                rows_s[i, :, at:end] = dot(sel[...], kept[i, at:end, :], ((1,), (1,))).astype(
                    jnp.bfloat16
                )

    here = pl.ds(pl.multiple_of(b * 2 * CAP, 16), 2 * CAP)
    for h, (rows, head) in enumerate(((rows_t, head_t), (rows_s, head_s))):
        lines = rows[:, here, :].reshape(count * 2 * CAP, rows.shape[-1])
        product = dot(lines, head[...], ((1,), (0,)))
        for i in range(count):
            for k in range(2):
                at = (2 * i + k) * CAP
                values, power = coded(product[at : at + CAP, k * BLOCK : (k + 1) * BLOCK])
                outs[i][0, h, pl.ds(pl.multiple_of((2 * b + k) * CAP, 16), CAP), :] = values
                powers[2 * i + h, pl.ds(2 * b + k, 1), :] = power

    @pl.when(b == pl.num_programs(0) - 1)
    def _():
        for i in range(count):
            for h in range(2):
                outs[i][0, h, blocks * CAP :, :] = (
                    powers[2 * i + h].astype(jnp.int32).astype(jnp.int16)
                )


def partial_logits(meta, pos, steps, mine, others, head_t, head_s):
    count = len(steps)
    tokens = pos.shape[-1]
    deep_t, width = head_t.shape
    deep_s = head_s.shape[0]
    blocks = width // BLOCK
    coded_rows = blocks * CAP + 16
    whole = lambda a: pl.BlockSpec(a.shape, lambda b, meta: (0,) * a.ndim)
    return pl.pallas_call(
        functools.partial(partial_kernel, steps),
        name="partial_logits",
        grid_spec=pltpu.PrefetchScalarGridSpec(
            num_scalar_prefetch=1,
            grid=(blocks // 2,),
            in_specs=[whole(pos)]
            + [whole(a) for a in (*mine, *others)]
            + [
                pl.BlockSpec((deep_t, 2 * BLOCK), lambda b, meta: (0, b)),
                pl.BlockSpec((deep_s, 2 * BLOCK), lambda b, meta: (0, b)),
            ],
            out_specs=[pl.BlockSpec((1, 2, coded_rows, BLOCK), lambda b, meta: (0, 0, 0, 0))] * count
            + [pl.BlockSpec((count, deep_s, tokens), lambda b, meta: (0, 0, 0))],
            scratch_shapes=[
                pltpu.VMEM((blocks * CAP, tokens), jnp.bfloat16),
                pltpu.VMEM((count, blocks * CAP, deep_t), jnp.bfloat16),
                pltpu.VMEM((count, blocks * CAP, deep_s), jnp.bfloat16),
                pltpu.VMEM((2 * count, 16, BLOCK), jnp.float32),
            ],
        ),
        out_shape=[jax.ShapeDtypeStruct((1, 2, coded_rows, BLOCK), jnp.int16)] * count
        + [jax.ShapeDtypeStruct((count, deep_s, tokens), jnp.bfloat16)],
        compiler_params=params(),
        cost_estimate=pl.CostEstimate(
            flops=8 * count * blocks * CAP * (deep_t + deep_s) * tokens,
            bytes_accessed=2 * (deep_t + deep_s) * (width + count * tokens),
            transcendentals=0,
        ),
    )(meta, pos, *mine, *others, head_t, head_s)


def spread(mark, line):
    return jnp.sum(jnp.where(mark, line, jnp.zeros_like(line)), axis=1, keepdims=True)


def fold(mark, column):
    return jnp.sum(jnp.where(mark, column, jnp.zeros_like(column)), axis=0, keepdims=True)


def unpacked(ref, h, blocks):
    powers = ref[0, h, blocks * CAP :, :].astype(jnp.int32).astype(jnp.float32)
    return [
        decoded(ref[0, h, b * CAP : (b + 1) * CAP, :], powers[b : b + 1, :]) for b in range(blocks)
    ]


def early_kernel(a0, a1, a2, total):
    blocks = total.shape[1]
    for h in range(2):
        for b, (x, y, z) in enumerate(zip(*(unpacked(a, h, blocks) for a in (a0, a1, a2)))):
            total[h, b] = x + y + z


def early_sum(parts):
    blocks = parts[0].shape[2] // CAP
    return pl.pallas_call(
        early_kernel,
        name="early_sum",
        out_shape=jax.ShapeDtypeStruct((2, blocks, CAP, BLOCK), jnp.float32),
        compiler_params=params(),
    )(*parts)


def stats_kernel(pos, target, places, early, last, logits, stats):
    blocks = logits.shape[1]
    tokens = pos.shape[-1]
    tops = [jnp.full((1, tokens), NEG, jnp.float32) for _ in range(2)]
    for h in range(2):
        for b, part in enumerate(unpacked(last, h, blocks)):
            total = early[h, b] + part
            logits[h, b] = total
            peak = jnp.max(total, axis=1, keepdims=True)
            mark = selector(pos[b : b + 1, :])
            tops[h] = jnp.maximum(
                tops[h], jnp.max(jnp.where(mark, peak, NEG), axis=0, keepdims=True)
            )
    zero = jnp.zeros((1, tokens), jnp.float32)
    sum_t, cross, sum_s, picked = zero, zero, zero, zero
    lanes = lax.broadcasted_iota(jnp.int32, (CAP, BLOCK), 1)
    for b in range(blocks):
        mark = selector(pos[b : b + 1, :])
        lt, ls = logits[0, b], logits[1, b]
        et = jnp.exp(lt - spread(mark, tops[0]))
        es = jnp.exp(ls - spread(mark, tops[1]))
        wanted = spread(mark, target[...] - b * BLOCK)
        sum_t = sum_t + fold(mark, jnp.sum(et, axis=1, keepdims=True))
        cross = cross + fold(mark, jnp.sum(et * (lt - ls), axis=1, keepdims=True))
        sum_s = sum_s + fold(mark, jnp.sum(es, axis=1, keepdims=True))
        picked = picked + fold(
            mark, jnp.sum(jnp.where(lanes == wanted, ls, 0.0), axis=1, keepdims=True)
        )
    most = jnp.max(places[...].astype(jnp.float32), axis=(0, 1))[None]
    most = jnp.broadcast_to(jnp.max(most, axis=1, keepdims=True), zero.shape)
    lines = [tops[0], sum_t, cross, tops[1], sum_s, picked, most, zero]
    stats[...] = jnp.concatenate(lines, axis=0)


def row_stats(pos, target, places, early, last):
    return pl.pallas_call(
        stats_kernel,
        name="row_stats",
        out_shape=[
            jax.ShapeDtypeStruct(early.shape, jnp.float32),
            jax.ShapeDtypeStruct((8, pos.shape[-1]), jnp.float32),
        ],
        compiler_params=params(),
    )(pos, target, places, early, last)


def combined(seen):
    top_t = jnp.max(seen[:, 0, :], axis=0, keepdims=True)
    top_s = jnp.max(seen[:, 3, :], axis=0, keepdims=True)
    scale_t = jnp.exp(seen[:, 0, :] - top_t)
    scale_s = jnp.exp(seen[:, 3, :] - top_s)
    total = lambda a: jnp.sum(a, axis=0, keepdims=True)
    sum_t = total(seen[:, 1, :] * scale_t)
    cross = total(seen[:, 2, :] * scale_t)
    sum_s = total(seen[:, 4, :] * scale_s)
    picked = total(seen[:, 5, :])
    log_t = top_t + jnp.log(sum_t)
    log_s = top_s + jnp.log(sum_s)
    return top_t, sum_t, top_s, sum_s, cross / sum_t - log_t + log_s, picked - log_s


def grad_kernel(pos, seen, logits, grad, rows):
    top_t, sum_t, top_s, sum_s, row_kl, logprob = combined(seen[...])
    most = jnp.max(seen[:, 6, :], axis=0, keepdims=True)
    rows[...] = jnp.concatenate([row_kl, logprob, most] + [most] * 5, axis=0)
    inv_t, inv_s = 1.0 / sum_t, 1.0 / sum_s
    for b in range(logits.shape[1]):
        mark = selector(pos[b : b + 1, :])
        et = jnp.exp(logits[0, b] - spread(mark, top_t)) * spread(mark, inv_t)
        es = jnp.exp(logits[1, b] - spread(mark, top_s)) * spread(mark, inv_s)
        grad[b] = (es - et).astype(jnp.bfloat16)


def row_grads(pos, seen, logits):
    return pl.pallas_call(
        grad_kernel,
        name="row_grads",
        out_shape=[
            jax.ShapeDtypeStruct(logits.shape[1:], jnp.bfloat16),
            jax.ShapeDtypeStruct((8, pos.shape[-1]), jnp.float32),
        ],
        compiler_params=params(),
    )(pos, seen, logits)


def head_kernel(meta, places, *refs):
    *studs, out, left = refs
    grads, studs = studs[:4], studs[4:]
    tokens = places.shape[-1]
    b = pl.program_id(0)

    @pl.when(b == 0)
    def _():
        step = 1
        for ref in studs:
            for i in range(ref.shape[0]):
                at = pl.multiple_of(meta[step] * tokens, tokens)
                left[:, pl.ds(at, tokens)] = ref[i]
                step += 1

    right = []
    for t, grad in enumerate(grads):
        pair = []
        for k in range(2):
            mark = selector(places[t, 2 * b + k][None]).astype(jnp.float32).astype(jnp.bfloat16)
            pair.append(dot(mark, grad[k], ((0,), (0,))).astype(jnp.bfloat16))
        right.append(jnp.concatenate(pair, axis=1))
    out[...] = dot(left[...], jnp.concatenate(right, axis=0), ((1,), (0,)))


def head_gradient(meta, places, grads, studs):
    deep, tokens = studs[0].shape[1:]
    blocks = grads[0].shape[0]
    whole = lambda a: pl.BlockSpec(a.shape, lambda b, meta: (0,) * a.ndim)
    return pl.pallas_call(
        head_kernel,
        name="head_gradient",
        grid_spec=pltpu.PrefetchScalarGridSpec(
            num_scalar_prefetch=1,
            grid=(blocks // 2,),
            in_specs=[whole(places)]
            + [pl.BlockSpec((2, CAP, BLOCK), lambda b, meta: (b, 0, 0)) for _ in grads]
            + [whole(a) for a in studs],
            out_specs=pl.BlockSpec((deep, 2 * BLOCK), lambda b, meta: (0, b)),
            scratch_shapes=[pltpu.VMEM((deep, 4 * tokens), jnp.bfloat16)],
        ),
        out_shape=jax.ShapeDtypeStruct((deep, blocks * BLOCK), jnp.float32),
        compiler_params=params(),
    )(meta, places, *grads, *studs)


def build(sx, sz, sc):
    turn = lambda step: [
        (x * sx + y, ((y + step - x) % sx) * sx + y) for x in range(sx) for y in range(sx)
    ]
    spread_out = [(x * sx + y, y * sx + (x + y) % sx) for x in range(sx) for y in range(sx)]
    shift = lambda step: [(y, (y + step) % sx) for y in range(sx)]

    def to_owner(a, step):
        return lax.ppermute(a, ("x", "y"), turn(step))

    def both_cores(mine):
        if sc == 1:
            return mine[:, None]
        other = lax.ppermute(mine, "c", [(0, 1), (1, 0)])
        first = lax.axis_index("c") == 0
        return jnp.stack([jnp.where(first, mine, other), jnp.where(first, other, mine)], axis=1)

    def features(pay, tokens):
        full = both_cores(pay)
        chunks = full.shape[0] * full.shape[1]
        full = full.reshape(chunks, -1, BLOCK)
        teach = full[:, :tokens]
        stud = full[:, tokens:].reshape(chunks, tokens // BLOCK, -1, BLOCK)
        stud = stud.transpose(0, 2, 1, 3).reshape(-1, tokens)
        return teach, stud

    def neighbours(pay):
        after = lax.ppermute(pay, "y", shift(-1))
        before = lax.ppermute(pay, "y", shift(1))
        return after, before

    def opposite(pay):
        return lax.ppermute(pay, "y", shift(2))

    def everyone(stats):
        copies = jnp.broadcast_to(stats[None], (sx * sz * sc, *stats.shape))
        return lax.all_to_all(copies, LOCAL, split_axis=0, concat_axis=0, tiled=True)

    def dense(pays, head_t, head_s, allowed, target):
        tokens, blocks = allowed.shape
        width = head_t.shape[1]
        pairs = [features(pays[step], tokens) for step in range(sx)]
        teach = jnp.concatenate([t.transpose(1, 0, 2).reshape(tokens, -1) for t, _ in pairs])
        studs = jnp.concatenate([stud for _, stud in pairs], axis=1)
        part = jnp.concatenate(
            [dot(teach, head_t, ((1,), (0,))), dot(studs, head_s, ((0,), (0,)))], axis=1
        )
        total = sum(
            to_owner(part[step * tokens : (step + 1) * tokens], step) for step in range(sx)
        )
        lt, ls = total[:, :width], total[:, width:]
        open_ = jnp.broadcast_to((allowed > 0)[:, :, None], (tokens, blocks, BLOCK))
        open_ = open_.reshape(tokens, width)
        ids = jnp.arange(width, dtype=jnp.int32)
        picked = jnp.sum(jnp.where(ids[None, :] == target[:, None], ls, 0.0), axis=1)
        top_t = jnp.max(jnp.where(open_, lt, NEG), axis=1)
        top_s = jnp.max(jnp.where(open_, ls, NEG), axis=1)
        et = jnp.where(open_, jnp.exp(jnp.where(open_, lt, NEG) - top_t[:, None]), 0.0)
        es = jnp.where(open_, jnp.exp(jnp.where(open_, ls, NEG) - top_s[:, None]), 0.0)
        lines = [top_t, et.sum(1), (et * (lt - ls)).sum(1), top_s, es.sum(1), picked]
        stats = jnp.stack(lines + [jnp.zeros_like(top_t)] * 2)
        all_t, sum_t, all_s, sum_s, row_kl, logprob = combined(everyone(stats))
        scale_t = (jnp.exp(top_t[None] - all_t) / sum_t)[0]
        scale_s = (jnp.exp(top_s[None] - all_s) / sum_s)[0]
        grad = (es * scale_s[:, None] - et * scale_t[:, None]).astype(jnp.bfloat16)
        grads = jnp.concatenate([to_owner(grad, step) for step in range(sx)])
        head = dot(studs, grads, ((1,), (0,)))
        return row_kl[0], logprob[0], head

    def other_core(pay):
        return lax.ppermute(pay, "c", [(0, 1), (1, 0)]) if sc > 1 else pay

    def per_device(teacher_hidden, student_hidden, head_t, head_s, allowed, sampled):
        tokens, blocks = allowed.shape
        width = head_t.shape[1]
        stud = student_hidden.T.reshape(-1, tokens // BLOCK, BLOCK).transpose(1, 0, 2)
        pay = jnp.concatenate([teacher_hidden, stud.reshape(-1, BLOCK)], axis=0)
        pay = lax.ppermute(pay, ("x", "y"), spread_out)
        open_ = (allowed > 0).T.astype(jnp.float32)
        before = jnp.triu(jnp.ones((tokens, tokens), jnp.float32), 1)
        place = dot(open_.astype(jnp.bfloat16), before.astype(jnp.bfloat16), ((1,), (0,)))
        own_pos = jnp.where(open_ > 0, place.astype(jnp.int32), -1)
        own_pos = jnp.pad(own_pos, ((0, -blocks % 8), (0, 0)), constant_values=-1)
        order = (0, 1, 3, 2)

        def from_line(a, far):
            return lax.ppermute(a, "x", [(x, (x - far) % sx) for x in range(sx)])

        places = [own_pos] + [from_line(own_pos, far) for far in range(1, sx)]
        places = jnp.stack(places)
        pay = lax.all_to_all(jnp.broadcast_to(pay[None], (sz, *pay.shape)), "z", 0, 0, tiled=True)
        here, row, core = (lax.axis_index(name).astype(jnp.int32) for name in ("x", "y", "c"))
        meta = jnp.stack([core] + [(row + step - 2 * here) % sx for step in order])
        place_of = (row * sz + lax.axis_index("z")) * sc + core
        target = sampled - place_of * width

        def run(steps, mine, others):
            return partial_logits(meta, places, steps, mine, others, head_t, head_s)

        pay, other = lax.optimization_barrier((pay, other_core(pay)))
        after, ahead = neighbours(pay)
        part, stud0 = run((0,), [pay], [other])
        got = [to_owner(part, order[0])]
        far = opposite(pay)
        part, other_part, stud1 = run((1, 2), [after, ahead], [other_core(after), other_core(ahead)])
        got += [to_owner(part, order[1]), to_owner(other_part, order[2])]
        part, stud2 = run((3,), [far], [other_core(far)])
        got.append(to_owner(part, order[3]))

        early = early_sum(got[:3])
        logits, stats = row_stats(own_pos, target[None], places, early, got[3])
        grad, rows = row_grads(own_pos, everyone(stats), logits)
        grads = [grad] + [from_line(grad, far) for far in range(1, sx)]
        head = head_gradient(meta, places, grads, [stud0, stud1, stud2])
        start = (rows[2, 0] >= CAP, rows[0], rows[1], head)
        pays = {0: pay, 1: after, 3: ahead, 2: far}

        def redo(_):
            return (False, *dense(pays, head_t, head_s, allowed, target))

        return lax.while_loop(lambda held: held[0], redo, start)[1:]

    return per_device


def solution(mesh, sizes=(4, 8, 2)):
    sx, sz, sc = sizes
    grid = Mesh(mesh.devices.reshape(sx, sx, sz, sc), ("x", "y", "z", "c"))
    both = P("x", LOCAL)
    return jax.shard_map(
        build(sx, sz, sc),
        mesh=grid,
        in_specs=(both, both, both, both, both, P("x")),
        out_specs=(P("x"), P("x"), both),
        check_vma=False,
    )
```

```python
import functools

import jax
import jax.numpy as jnp
from jax import lax
from jax.experimental import pallas as pl
from jax.experimental.pallas import tpu as pltpu
from jax.sharding import Mesh
from jax.sharding import PartitionSpec as P

CAP = 80
NEG = -1e30
BLOCK = 128
LOCAL = ("y", "z", "c")


def dot(a, b, dims):
    return lax.dot_general(a, b, (dims, ((), ())), preferred_element_type=jnp.float32)


def params(**kw):
    return pltpu.CompilerParams(vmem_limit_bytes=36 << 20, **kw)


def selector(pos_row):
    lines = lax.broadcasted_iota(jnp.int32, (CAP, pos_row.shape[-1]), 0)
    return lines == pos_row


def diagonal():
    rows = lax.broadcasted_iota(jnp.int32, (CAP, BLOCK), 0)
    return rows == lax.broadcasted_iota(jnp.int32, (CAP, BLOCK), 1)


def coded(logits):
    peak = jnp.max(jnp.abs(logits), axis=1, keepdims=True)
    power = jnp.floor(jnp.log2(jnp.maximum(peak, 1e-30)))
    scaled = jnp.round(logits * jnp.exp2(14.0 - power))
    values = jnp.clip(scaled, -32767.0, 32767.0).astype(jnp.int32).astype(jnp.int16)
    return values, jnp.sum(jnp.where(diagonal(), power, 0.0), axis=0, keepdims=True)


def decoded(values, powers):
    power = jnp.sum(jnp.where(diagonal(), powers, 0.0), axis=1, keepdims=True)
    return values.astype(jnp.int32).astype(jnp.float32) * jnp.exp2(power - 14.0)


def partial_kernel(steps, meta, pos, *refs):
    count = len(steps)
    mine, others = refs[:count], refs[count : 2 * count]
    far_t, far_s = refs[2 * count : 2 * count + 2]
    outs = refs[2 * count + 2 : 3 * count + 2]
    kept, sel, rows_t, rows_s, powers, head_t, head_s, sems = refs[3 * count + 2 :]
    fetch_t = pltpu.make_async_copy(far_t, head_t, sems.at[0])
    fetch_s = pltpu.make_async_copy(far_s, head_s, sems.at[1])
    fetch_t.start()
    fetch_s.start()
    blocks = sel.shape[0] // CAP
    depth, tokens = mine[0].shape[0], sel.shape[1]
    both = kept.shape[1] // depth
    first = meta[0] == 0
    powers[...] = jnp.zeros_like(powers)
    for i in range(count):
        held = meta[1 + steps[i]]
        for k in range(blocks):
            mark = selector(pos[held, k : k + 1, :]).astype(jnp.float32)
            sel[k * CAP : (k + 1) * CAP, :] = mark.astype(jnp.bfloat16)

        def chunk(z, _, i=i):
            a, o = mine[i][z, :tokens, :], others[i][z, :tokens, :]
            pair = jnp.concatenate([jnp.where(first, a, o), jnp.where(first, o, a)], axis=1)
            rows_t[i, :, pl.ds(pl.multiple_of(z * 256, 256), 256)] = dot(
                sel[...], pair, ((1,), (0,))
            ).astype(jnp.bfloat16)
            a = mine[i][z, tokens:, :].astype(jnp.float32)
            o = others[i][z, tokens:, :].astype(jnp.float32)
            parts = []
            for part in (jnp.where(first, a, o), jnp.where(first, o, a)):
                parts.append(jnp.concatenate([part[: both // 2], part[both // 2 :]], axis=1))
            kept[i, pl.ds(pl.multiple_of(z * both, 16), both), :] = jnp.concatenate(
                parts, axis=0
            ).astype(jnp.bfloat16)
            return 0

        lax.fori_loop(0, depth, chunk, 0)
        deep_s = kept.shape[1]
        for at in range(0, deep_s, 256):
            end = min(at + 256, deep_s)
            rows_s[i, :, at:end] = dot(sel[...], kept[i, at:end, :], ((1,), (1,))).astype(
                jnp.bfloat16
            )

    def two_blocks(b, _):
        here = pl.ds(pl.multiple_of(b * 2 * CAP, 16), 2 * CAP)
        columns = pl.ds(pl.multiple_of(b * 2 * BLOCK, 2 * BLOCK), 2 * BLOCK)
        for h, (rows, head) in enumerate(((rows_t, head_t), (rows_s, head_s))):
            lines = rows[:, here, :].reshape(count * 2 * CAP, rows.shape[-1])
            product = dot(lines, head[:, columns], ((1,), (0,)))
            for i in range(count):
                for k in range(2):
                    at = (2 * i + k) * CAP
                    values, power = coded(product[at : at + CAP, k * BLOCK : (k + 1) * BLOCK])
                    outs[i][0, h, pl.ds(pl.multiple_of((2 * b + k) * CAP, 16), CAP), :] = values
                    powers[2 * i + h, pl.ds(2 * b + k, 1), :] = power
        return 0

    fetch_t.wait()
    fetch_s.wait()
    lax.fori_loop(0, blocks // 2, two_blocks, 0)
    for i in range(count):
        for h in range(2):
            outs[i][0, h, blocks * CAP :, :] = powers[2 * i + h].astype(jnp.int32).astype(jnp.int16)


def partial_logits(meta, pos, steps, mine, others, head_t, head_s):
    count = len(steps)
    tokens = pos.shape[-1]
    deep_t, width = head_t.shape
    deep_s = head_s.shape[0]
    blocks = width // BLOCK
    coded_rows = blocks * CAP + 16
    return pl.pallas_call(
        functools.partial(partial_kernel, steps),
        name="partial_logits",
        in_specs=[pl.BlockSpec(memory_space=pltpu.SMEM)]
        + [pl.BlockSpec(memory_space=pltpu.VMEM)] * (2 * count + 1)
        + [pl.BlockSpec(memory_space=pl.ANY)] * 2,
        scratch_shapes=[
            pltpu.VMEM((blocks * CAP, tokens), jnp.bfloat16),
            pltpu.VMEM((count, blocks * CAP, deep_t), jnp.bfloat16),
            pltpu.VMEM((count, blocks * CAP, deep_s), jnp.bfloat16),
            pltpu.VMEM((2 * count, 16, BLOCK), jnp.float32),
            pltpu.VMEM(head_t.shape, head_t.dtype),
            pltpu.VMEM(head_s.shape, head_s.dtype),
            pltpu.SemaphoreType.DMA((2,)),
        ],
        out_shape=[jax.ShapeDtypeStruct((1, 2, coded_rows, BLOCK), jnp.int16)] * count
        + [jax.ShapeDtypeStruct((count, deep_s, tokens), jnp.bfloat16)],
        compiler_params=params(),
        cost_estimate=pl.CostEstimate(
            flops=8 * count * blocks * CAP * (deep_t + deep_s) * tokens,
            bytes_accessed=2 * (deep_t + deep_s) * (width + count * tokens),
            transcendentals=0,
        ),
    )(meta, pos, *mine, *others, head_t, head_s)


def spread(mark, line):
    return jnp.sum(jnp.where(mark, line, jnp.zeros_like(line)), axis=1, keepdims=True)


def fold(mark, column):
    return jnp.sum(jnp.where(mark, column, jnp.zeros_like(column)), axis=0, keepdims=True)


def unpacked(ref, h, blocks):
    powers = ref[0, h, blocks * CAP :, :].astype(jnp.int32).astype(jnp.float32)
    return [
        decoded(ref[0, h, b * CAP : (b + 1) * CAP, :], powers[b : b + 1, :]) for b in range(blocks)
    ]


def early_kernel(a0, a1, a2, total):
    blocks = total.shape[1]
    for h in range(2):
        for b, (x, y, z) in enumerate(zip(*(unpacked(a, h, blocks) for a in (a0, a1, a2)))):
            total[h, b] = x + y + z


def early_sum(parts):
    blocks = parts[0].shape[2] // CAP
    return pl.pallas_call(
        early_kernel,
        name="early_sum",
        out_shape=jax.ShapeDtypeStruct((2, blocks, CAP, BLOCK), jnp.float32),
        compiler_params=params(),
    )(*parts)


def stats_kernel(pos, target, places, early, last, logits, stats):
    blocks = logits.shape[1]
    tokens = pos.shape[-1]
    tops = [jnp.full((1, tokens), NEG, jnp.float32) for _ in range(2)]
    for h in range(2):
        for b, part in enumerate(unpacked(last, h, blocks)):
            total = early[h, b] + part
            logits[h, b] = total
            peak = jnp.max(total, axis=1, keepdims=True)
            mark = selector(pos[b : b + 1, :])
            tops[h] = jnp.maximum(
                tops[h], jnp.max(jnp.where(mark, peak, NEG), axis=0, keepdims=True)
            )
    zero = jnp.zeros((1, tokens), jnp.float32)
    sum_t, cross, sum_s, picked = zero, zero, zero, zero
    lanes = lax.broadcasted_iota(jnp.int32, (CAP, BLOCK), 1)
    for b in range(blocks):
        mark = selector(pos[b : b + 1, :])
        lt, ls = logits[0, b], logits[1, b]
        et = jnp.exp(lt - spread(mark, tops[0]))
        es = jnp.exp(ls - spread(mark, tops[1]))
        wanted = spread(mark, target[...] - b * BLOCK)
        sum_t = sum_t + fold(mark, jnp.sum(et, axis=1, keepdims=True))
        cross = cross + fold(mark, jnp.sum(et * (lt - ls), axis=1, keepdims=True))
        sum_s = sum_s + fold(mark, jnp.sum(es, axis=1, keepdims=True))
        picked = picked + fold(
            mark, jnp.sum(jnp.where(lanes == wanted, ls, 0.0), axis=1, keepdims=True)
        )
    most = jnp.max(places[...].astype(jnp.float32), axis=(0, 1))[None]
    most = jnp.broadcast_to(jnp.max(most, axis=1, keepdims=True), zero.shape)
    lines = [tops[0], sum_t, cross, tops[1], sum_s, picked, most, zero]
    stats[...] = jnp.concatenate(lines, axis=0)


def row_stats(pos, target, places, early, last):
    return pl.pallas_call(
        stats_kernel,
        name="row_stats",
        out_shape=[
            jax.ShapeDtypeStruct(early.shape, jnp.float32),
            jax.ShapeDtypeStruct((8, pos.shape[-1]), jnp.float32),
        ],
        compiler_params=params(),
    )(pos, target, places, early, last)


def combined(seen):
    top_t = jnp.max(seen[:, 0, :], axis=0, keepdims=True)
    top_s = jnp.max(seen[:, 3, :], axis=0, keepdims=True)
    scale_t = jnp.exp(seen[:, 0, :] - top_t)
    scale_s = jnp.exp(seen[:, 3, :] - top_s)
    total = lambda a: jnp.sum(a, axis=0, keepdims=True)
    sum_t = total(seen[:, 1, :] * scale_t)
    cross = total(seen[:, 2, :] * scale_t)
    sum_s = total(seen[:, 4, :] * scale_s)
    picked = total(seen[:, 5, :])
    log_t = top_t + jnp.log(sum_t)
    log_s = top_s + jnp.log(sum_s)
    return top_t, sum_t, top_s, sum_s, cross / sum_t - log_t + log_s, picked - log_s


def grad_kernel(pos, seen, logits, grad, rows):
    top_t, sum_t, top_s, sum_s, row_kl, logprob = combined(seen[...])
    most = jnp.max(seen[:, 6, :], axis=0, keepdims=True)
    rows[...] = jnp.concatenate([row_kl, logprob, most] + [most] * 5, axis=0)
    inv_t, inv_s = 1.0 / sum_t, 1.0 / sum_s
    for b in range(logits.shape[1]):
        mark = selector(pos[b : b + 1, :])
        et = jnp.exp(logits[0, b] - spread(mark, top_t)) * spread(mark, inv_t)
        es = jnp.exp(logits[1, b] - spread(mark, top_s)) * spread(mark, inv_s)
        grad[b] = (es - et).astype(jnp.bfloat16)


def row_grads(pos, seen, logits):
    return pl.pallas_call(
        grad_kernel,
        name="row_grads",
        out_shape=[
            jax.ShapeDtypeStruct(logits.shape[1:], jnp.bfloat16),
            jax.ShapeDtypeStruct((8, pos.shape[-1]), jnp.float32),
        ],
        compiler_params=params(),
    )(pos, seen, logits)


def head_kernel(meta, places, *refs):
    *studs, out, left = refs
    grads, studs = studs[:4], studs[4:]
    tokens = places.shape[-1]
    b = pl.program_id(0)

    @pl.when(b == 0)
    def _():
        step = 1
        for ref in studs:
            for i in range(ref.shape[0]):
                at = pl.multiple_of(meta[step] * tokens, tokens)
                left[:, pl.ds(at, tokens)] = ref[i]
                step += 1

    right = []
    for t, grad in enumerate(grads):
        pair = []
        for k in range(2):
            mark = selector(places[t, 2 * b + k][None]).astype(jnp.float32).astype(jnp.bfloat16)
            pair.append(dot(mark, grad[k], ((0,), (0,))).astype(jnp.bfloat16))
        right.append(jnp.concatenate(pair, axis=1))
    out[...] = dot(left[...], jnp.concatenate(right, axis=0), ((1,), (0,)))


def head_gradient(meta, places, grads, studs):
    deep, tokens = studs[0].shape[1:]
    blocks = grads[0].shape[0]
    whole = lambda a: pl.BlockSpec(a.shape, lambda b, meta: (0,) * a.ndim)
    return pl.pallas_call(
        head_kernel,
        name="head_gradient",
        grid_spec=pltpu.PrefetchScalarGridSpec(
            num_scalar_prefetch=1,
            grid=(blocks // 2,),
            in_specs=[whole(places)]
            + [pl.BlockSpec((2, CAP, BLOCK), lambda b, meta: (b, 0, 0)) for _ in grads]
            + [whole(a) for a in studs],
            out_specs=pl.BlockSpec((deep, 2 * BLOCK), lambda b, meta: (0, b)),
            scratch_shapes=[pltpu.VMEM((deep, 4 * tokens), jnp.bfloat16)],
        ),
        out_shape=jax.ShapeDtypeStruct((deep, blocks * BLOCK), jnp.float32),
        compiler_params=params(),
    )(meta, places, *grads, *studs)


def build(sx, sz, sc):
    turn = lambda step: [
        (x * sx + y, ((y + step - x) % sx) * sx + y) for x in range(sx) for y in range(sx)
    ]
    spread_out = [(x * sx + y, y * sx + (x + y) % sx) for x in range(sx) for y in range(sx)]
    shift = lambda step: [(y, (y + step) % sx) for y in range(sx)]

    def to_owner(a, step):
        return lax.ppermute(a, ("x", "y"), turn(step))

    def both_cores(mine):
        if sc == 1:
            return mine[:, None]
        other = lax.ppermute(mine, "c", [(0, 1), (1, 0)])
        first = lax.axis_index("c") == 0
        return jnp.stack([jnp.where(first, mine, other), jnp.where(first, other, mine)], axis=1)

    def features(pay, tokens):
        full = both_cores(pay)
        chunks = full.shape[0] * full.shape[1]
        full = full.reshape(chunks, -1, BLOCK)
        teach = full[:, :tokens]
        stud = full[:, tokens:].reshape(chunks, tokens // BLOCK, -1, BLOCK)
        stud = stud.transpose(0, 2, 1, 3).reshape(-1, tokens)
        return teach, stud

    def neighbours(pay):
        after = lax.ppermute(pay, "y", shift(-1))
        before = lax.ppermute(pay, "y", shift(1))
        return after, before

    def opposite(pay):
        return lax.ppermute(pay, "y", shift(2))

    def everyone(stats):
        copies = jnp.broadcast_to(stats[None], (sx * sz * sc, *stats.shape))
        return lax.all_to_all(copies, LOCAL, split_axis=0, concat_axis=0, tiled=True)

    def dense(pays, head_t, head_s, allowed, target):
        tokens, blocks = allowed.shape
        width = head_t.shape[1]
        pairs = [features(pays[step], tokens) for step in range(sx)]
        teach = jnp.concatenate([t.transpose(1, 0, 2).reshape(tokens, -1) for t, _ in pairs])
        studs = jnp.concatenate([stud for _, stud in pairs], axis=1)
        part = jnp.concatenate(
            [dot(teach, head_t, ((1,), (0,))), dot(studs, head_s, ((0,), (0,)))], axis=1
        )
        total = sum(
            to_owner(part[step * tokens : (step + 1) * tokens], step) for step in range(sx)
        )
        lt, ls = total[:, :width], total[:, width:]
        open_ = jnp.broadcast_to((allowed > 0)[:, :, None], (tokens, blocks, BLOCK))
        open_ = open_.reshape(tokens, width)
        ids = jnp.arange(width, dtype=jnp.int32)
        picked = jnp.sum(jnp.where(ids[None, :] == target[:, None], ls, 0.0), axis=1)
        top_t = jnp.max(jnp.where(open_, lt, NEG), axis=1)
        top_s = jnp.max(jnp.where(open_, ls, NEG), axis=1)
        et = jnp.where(open_, jnp.exp(jnp.where(open_, lt, NEG) - top_t[:, None]), 0.0)
        es = jnp.where(open_, jnp.exp(jnp.where(open_, ls, NEG) - top_s[:, None]), 0.0)
        lines = [top_t, et.sum(1), (et * (lt - ls)).sum(1), top_s, es.sum(1), picked]
        stats = jnp.stack(lines + [jnp.zeros_like(top_t)] * 2)
        all_t, sum_t, all_s, sum_s, row_kl, logprob = combined(everyone(stats))
        scale_t = (jnp.exp(top_t[None] - all_t) / sum_t)[0]
        scale_s = (jnp.exp(top_s[None] - all_s) / sum_s)[0]
        grad = (es * scale_s[:, None] - et * scale_t[:, None]).astype(jnp.bfloat16)
        grads = jnp.concatenate([to_owner(grad, step) for step in range(sx)])
        head = dot(studs, grads, ((1,), (0,)))
        return row_kl[0], logprob[0], head

    def other_core(pay):
        return lax.ppermute(pay, "c", [(0, 1), (1, 0)]) if sc > 1 else pay

    def per_device(teacher_hidden, student_hidden, head_t, head_s, allowed, sampled):
        tokens, blocks = allowed.shape
        width = head_t.shape[1]
        stud = student_hidden.T.reshape(-1, tokens // BLOCK, BLOCK).transpose(1, 0, 2)
        pay = jnp.concatenate([teacher_hidden, stud.reshape(-1, BLOCK)], axis=0)
        pay = lax.ppermute(pay, ("x", "y"), spread_out)
        open_ = (allowed > 0).T.astype(jnp.float32)
        before = jnp.triu(jnp.ones((tokens, tokens), jnp.float32), 1)
        place = dot(open_.astype(jnp.bfloat16), before.astype(jnp.bfloat16), ((1,), (0,)))
        own_pos = jnp.where(open_ > 0, place.astype(jnp.int32), -1)
        own_pos = jnp.pad(own_pos, ((0, -blocks % 8), (0, 0)), constant_values=-1)
        order = (0, 1, 3, 2)

        def from_line(a, far):
            return lax.ppermute(a, "x", [(x, (x - far) % sx) for x in range(sx)])

        places = [own_pos] + [from_line(own_pos, far) for far in range(1, sx)]
        places = jnp.stack(places)
        pay = lax.all_to_all(jnp.broadcast_to(pay[None], (sz, *pay.shape)), "z", 0, 0, tiled=True)
        here, row, core = (lax.axis_index(name).astype(jnp.int32) for name in ("x", "y", "c"))
        meta = jnp.stack([core] + [(row + step - 2 * here) % sx for step in order])
        place_of = (row * sz + lax.axis_index("z")) * sc + core
        target = sampled - place_of * width

        def run(steps, mine, others):
            return partial_logits(meta, places, steps, mine, others, head_t, head_s)

        pay, other = lax.optimization_barrier((pay, other_core(pay)))
        after, ahead = neighbours(pay)
        part, stud0 = run((0,), [pay], [other])
        got = [to_owner(part, order[0])]
        far = opposite(pay)
        part, other_part, stud1 = run((1, 2), [after, ahead], [other_core(after), other_core(ahead)])
        got += [to_owner(part, order[1]), to_owner(other_part, order[2])]
        part, stud2 = run((3,), [far], [other_core(far)])
        got.append(to_owner(part, order[3]))

        early = early_sum(got[:3])
        logits, stats = row_stats(own_pos, target[None], places, early, got[3])
        grad, rows = row_grads(own_pos, everyone(stats), logits)
        grads = [grad] + [from_line(grad, far) for far in range(1, sx)]
        head = head_gradient(meta, places, grads, [stud0, stud1, stud2])
        start = (rows[2, 0] >= CAP, rows[0], rows[1], head)
        pays = {0: pay, 1: after, 3: ahead, 2: far}

        def redo(_):
            return (False, *dense(pays, head_t, head_s, allowed, target))

        return lax.while_loop(lambda held: held[0], redo, start)[1:]

    return per_device


def solution(mesh, sizes=(4, 8, 2)):
    sx, sz, sc = sizes
    grid = Mesh(mesh.devices.reshape(sx, sx, sz, sc), ("x", "y", "z", "c"))
    both = P("x", LOCAL)
    return jax.shard_map(
        build(sx, sz, sc),
        mesh=grid,
        in_specs=(both, both, both, both, both, P("x")),
        out_specs=(P("x"), P("x"), both),
        check_vma=False,
    )
```

```python
import functools

import jax
import jax.numpy as jnp
from jax import lax
from jax.experimental import pallas as pl
from jax.experimental.pallas import tpu as pltpu
from jax.sharding import Mesh
from jax.sharding import PartitionSpec as P

CAP = 80
NEG = -1e30
BLOCK = 128
LOCAL = ("y", "z", "c")


def dot(a, b, dims):
    return lax.dot_general(a, b, (dims, ((), ())), preferred_element_type=jnp.float32)


def params(**kw):
    return pltpu.CompilerParams(vmem_limit_bytes=36 << 20, **kw)


def selector(pos_row):
    lines = lax.broadcasted_iota(jnp.int32, (CAP, pos_row.shape[-1]), 0)
    return lines == pos_row


def diagonal():
    rows = lax.broadcasted_iota(jnp.int32, (CAP, BLOCK), 0)
    return rows == lax.broadcasted_iota(jnp.int32, (CAP, BLOCK), 1)


def coded(logits):
    peak = jnp.max(jnp.abs(logits), axis=1, keepdims=True)
    power = jnp.floor(jnp.log2(jnp.maximum(peak, 1e-30)))
    scaled = jnp.round(logits * jnp.exp2(14.0 - power))
    values = jnp.clip(scaled, -32767.0, 32767.0).astype(jnp.int32).astype(jnp.int16)
    return values, jnp.sum(jnp.where(diagonal(), power, 0.0), axis=0, keepdims=True)


def decoded(values, powers):
    power = jnp.sum(jnp.where(diagonal(), powers, 0.0), axis=1, keepdims=True)
    return values.astype(jnp.int32).astype(jnp.float32) * jnp.exp2(power - 14.0)


def partial_kernel(steps, meta, pos, *refs):
    count = len(steps)
    mine, others = refs[:count], refs[count : 2 * count]
    far_t, far_s = refs[2 * count : 2 * count + 2]
    outs = refs[2 * count + 2 : 3 * count + 2]
    kept, sel, rows_t, rows_s, powers, head_t, head_s, sems = refs[3 * count + 2 :]
    fetch_t = pltpu.make_async_copy(far_t, head_t, sems.at[0])
    fetch_s = pltpu.make_async_copy(far_s, head_s, sems.at[1])
    fetch_t.start()
    fetch_s.start()
    blocks = sel.shape[0] // CAP
    depth, tokens = mine[0].shape[0], sel.shape[1]
    both = kept.shape[1] // depth
    first = meta[0] == 0
    powers[...] = jnp.zeros_like(powers)
    for i in range(count):
        held = meta[1 + steps[i]]
        for k in range(blocks):
            mark = selector(pos[held, k : k + 1, :]).astype(jnp.float32)
            sel[k * CAP : (k + 1) * CAP, :] = mark.astype(jnp.bfloat16)

        def chunk(z, _, i=i):
            a, o = mine[i][z, :tokens, :], others[i][z, :tokens, :]
            pair = jnp.concatenate([jnp.where(first, a, o), jnp.where(first, o, a)], axis=1)
            rows_t[i, :, pl.ds(pl.multiple_of(z * 256, 256), 256)] = dot(
                sel[...], pair, ((1,), (0,))
            ).astype(jnp.bfloat16)
            a = mine[i][z, tokens:, :].astype(jnp.float32)
            o = others[i][z, tokens:, :].astype(jnp.float32)
            parts = []
            for part in (jnp.where(first, a, o), jnp.where(first, o, a)):
                parts.append(jnp.concatenate([part[: both // 2], part[both // 2 :]], axis=1))
            kept[i, pl.ds(pl.multiple_of(z * both, 16), both), :] = jnp.concatenate(
                parts, axis=0
            ).astype(jnp.bfloat16)
            return 0

        lax.fori_loop(0, depth, chunk, 0)
        deep_s = kept.shape[1]
        for at in range(0, deep_s, 256):
            end = min(at + 256, deep_s)
            rows_s[i, :, at:end] = dot(sel[...], kept[i, at:end, :], ((1,), (1,))).astype(
                jnp.bfloat16
            )

    def two_blocks(b, _):
        here = pl.ds(pl.multiple_of(b * 2 * CAP, 16), 2 * CAP)
        columns = pl.ds(pl.multiple_of(b * 2 * BLOCK, 2 * BLOCK), 2 * BLOCK)
        for h, (rows, head) in enumerate(((rows_t, head_t), (rows_s, head_s))):
            lines = rows[:, here, :].reshape(count * 2 * CAP, rows.shape[-1])
            product = dot(lines, head[:, columns], ((1,), (0,)))
            for i in range(count):
                for k in range(2):
                    at = (2 * i + k) * CAP
                    values, power = coded(product[at : at + CAP, k * BLOCK : (k + 1) * BLOCK])
                    outs[i][0, h, pl.ds(pl.multiple_of((2 * b + k) * CAP, 16), CAP), :] = values
                    powers[2 * i + h, pl.ds(2 * b + k, 1), :] = power
        return 0

    fetch_t.wait()
    fetch_s.wait()
    lax.fori_loop(0, blocks // 2, two_blocks, 0)
    for i in range(count):
        for h in range(2):
            outs[i][0, h, blocks * CAP :, :] = powers[2 * i + h].astype(jnp.int32).astype(jnp.int16)


def partial_logits(meta, pos, steps, mine, others, head_t, head_s):
    count = len(steps)
    tokens = pos.shape[-1]
    deep_t, width = head_t.shape
    deep_s = head_s.shape[0]
    blocks = width // BLOCK
    coded_rows = blocks * CAP + 16
    return pl.pallas_call(
        functools.partial(partial_kernel, steps),
        name="partial_logits",
        in_specs=[pl.BlockSpec(memory_space=pltpu.SMEM)]
        + [pl.BlockSpec(memory_space=pltpu.VMEM)] * (2 * count + 1)
        + [pl.BlockSpec(memory_space=pl.ANY)] * 2,
        scratch_shapes=[
            pltpu.VMEM((blocks * CAP, tokens), jnp.bfloat16),
            pltpu.VMEM((count, blocks * CAP, deep_t), jnp.bfloat16),
            pltpu.VMEM((count, blocks * CAP, deep_s), jnp.bfloat16),
            pltpu.VMEM((2 * count, 16, BLOCK), jnp.float32),
            pltpu.VMEM(head_t.shape, head_t.dtype),
            pltpu.VMEM(head_s.shape, head_s.dtype),
            pltpu.SemaphoreType.DMA((2,)),
        ],
        out_shape=[jax.ShapeDtypeStruct((1, 2, coded_rows, BLOCK), jnp.int16)] * count
        + [jax.ShapeDtypeStruct((count, deep_s, tokens), jnp.bfloat16)],
        compiler_params=params(),
        cost_estimate=pl.CostEstimate(
            flops=8 * count * blocks * CAP * (deep_t + deep_s) * tokens,
            bytes_accessed=2 * (deep_t + deep_s) * (width + count * tokens),
            transcendentals=0,
        ),
    )(meta, pos, *mine, *others, head_t, head_s)


def spread(mark, line):
    return jnp.sum(jnp.where(mark, line, jnp.zeros_like(line)), axis=1, keepdims=True)


def fold(mark, column):
    return jnp.sum(jnp.where(mark, column, jnp.zeros_like(column)), axis=0, keepdims=True)


def unpacked(ref, h, blocks):
    powers = ref[0, h, blocks * CAP :, :].astype(jnp.int32).astype(jnp.float32)
    return [
        decoded(ref[0, h, b * CAP : (b + 1) * CAP, :], powers[b : b + 1, :]) for b in range(blocks)
    ]


def early_kernel(a0, a1, a2, total):
    blocks = total.shape[1]
    for h in range(2):
        for b, (x, y, z) in enumerate(zip(*(unpacked(a, h, blocks) for a in (a0, a1, a2)))):
            total[h, b] = x + y + z


def early_sum(parts):
    blocks = parts[0].shape[2] // CAP
    return pl.pallas_call(
        early_kernel,
        name="early_sum",
        out_shape=jax.ShapeDtypeStruct((2, blocks, CAP, BLOCK), jnp.float32),
        compiler_params=params(),
    )(*parts)


def stats_kernel(pos, target, places, early, last, logits, stats):
    blocks = logits.shape[1]
    tokens = pos.shape[-1]
    tops = [jnp.full((1, tokens), NEG, jnp.float32) for _ in range(2)]
    for h in range(2):
        for b, part in enumerate(unpacked(last, h, blocks)):
            total = early[h, b] + part
            logits[h, b] = total
            peak = jnp.max(total, axis=1, keepdims=True)
            mark = selector(pos[b : b + 1, :])
            tops[h] = jnp.maximum(
                tops[h], jnp.max(jnp.where(mark, peak, NEG), axis=0, keepdims=True)
            )
    zero = jnp.zeros((1, tokens), jnp.float32)
    sum_t, cross, sum_s, picked = zero, zero, zero, zero
    lanes = lax.broadcasted_iota(jnp.int32, (CAP, BLOCK), 1)
    for b in range(blocks):
        mark = selector(pos[b : b + 1, :])
        lt, ls = logits[0, b], logits[1, b]
        et = jnp.exp(lt - spread(mark, tops[0]))
        es = jnp.exp(ls - spread(mark, tops[1]))
        wanted = spread(mark, target[...] - b * BLOCK)
        sum_t = sum_t + fold(mark, jnp.sum(et, axis=1, keepdims=True))
        cross = cross + fold(mark, jnp.sum(et * (lt - ls), axis=1, keepdims=True))
        sum_s = sum_s + fold(mark, jnp.sum(es, axis=1, keepdims=True))
        picked = picked + fold(
            mark, jnp.sum(jnp.where(lanes == wanted, ls, 0.0), axis=1, keepdims=True)
        )
    most = jnp.max(places[...].astype(jnp.float32), axis=(0, 1))[None]
    most = jnp.broadcast_to(jnp.max(most, axis=1, keepdims=True), zero.shape)
    lines = [tops[0], sum_t, cross, tops[1], sum_s, picked, most, zero]
    stats[...] = jnp.concatenate(lines, axis=0)


def row_stats(pos, target, places, early, last):
    return pl.pallas_call(
        stats_kernel,
        name="row_stats",
        out_shape=[
            jax.ShapeDtypeStruct(early.shape, jnp.float32),
            jax.ShapeDtypeStruct((8, pos.shape[-1]), jnp.float32),
        ],
        compiler_params=params(),
    )(pos, target, places, early, last)


def combined(seen):
    top_t = jnp.max(seen[:, 0, :], axis=0, keepdims=True)
    top_s = jnp.max(seen[:, 3, :], axis=0, keepdims=True)
    scale_t = jnp.exp(seen[:, 0, :] - top_t)
    scale_s = jnp.exp(seen[:, 3, :] - top_s)
    total = lambda a: jnp.sum(a, axis=0, keepdims=True)
    sum_t = total(seen[:, 1, :] * scale_t)
    cross = total(seen[:, 2, :] * scale_t)
    sum_s = total(seen[:, 4, :] * scale_s)
    picked = total(seen[:, 5, :])
    log_t = top_t + jnp.log(sum_t)
    log_s = top_s + jnp.log(sum_s)
    return top_t, sum_t, top_s, sum_s, cross / sum_t - log_t + log_s, picked - log_s


def grad_kernel(pos, seen, logits, grad, rows):
    top_t, sum_t, top_s, sum_s, row_kl, logprob = combined(seen[...])
    most = jnp.max(seen[:, 6, :], axis=0, keepdims=True)
    rows[...] = jnp.concatenate([row_kl, logprob, most] + [most] * 5, axis=0)
    inv_t, inv_s = 1.0 / sum_t, 1.0 / sum_s
    for b in range(logits.shape[1]):
        mark = selector(pos[b : b + 1, :])
        et = jnp.exp(logits[0, b] - spread(mark, top_t)) * spread(mark, inv_t)
        es = jnp.exp(logits[1, b] - spread(mark, top_s)) * spread(mark, inv_s)
        grad[b] = (es - et).astype(jnp.bfloat16)


def row_grads(pos, seen, logits):
    return pl.pallas_call(
        grad_kernel,
        name="row_grads",
        out_shape=[
            jax.ShapeDtypeStruct(logits.shape[1:], jnp.bfloat16),
            jax.ShapeDtypeStruct((8, pos.shape[-1]), jnp.float32),
        ],
        compiler_params=params(),
    )(pos, seen, logits)


def head_kernel(meta, places, *refs):
    *studs, out, left = refs
    grads, studs = studs[:4], studs[4:]
    tokens = places.shape[-1]
    b = pl.program_id(0)

    @pl.when(b == 0)
    def _():
        step = 1
        for ref in studs:
            for i in range(ref.shape[0]):
                at = pl.multiple_of(meta[step] * tokens, tokens)
                left[:, pl.ds(at, tokens)] = ref[i]
                step += 1

    right = []
    for t, grad in enumerate(grads):
        pair = []
        for k in range(2):
            mark = selector(places[t, 2 * b + k][None]).astype(jnp.float32).astype(jnp.bfloat16)
            pair.append(dot(mark, grad[k], ((0,), (0,))).astype(jnp.bfloat16))
        right.append(jnp.concatenate(pair, axis=1))
    out[...] = dot(left[...], jnp.concatenate(right, axis=0), ((1,), (0,)))


def head_gradient(meta, places, grads, studs):
    deep, tokens = studs[0].shape[1:]
    blocks = grads[0].shape[0]
    whole = lambda a: pl.BlockSpec(a.shape, lambda b, meta: (0,) * a.ndim)
    return pl.pallas_call(
        head_kernel,
        name="head_gradient",
        grid_spec=pltpu.PrefetchScalarGridSpec(
            num_scalar_prefetch=1,
            grid=(blocks // 2,),
            in_specs=[whole(places)]
            + [pl.BlockSpec((2, CAP, BLOCK), lambda b, meta: (b, 0, 0)) for _ in grads]
            + [whole(a) for a in studs],
            out_specs=pl.BlockSpec((deep, 2 * BLOCK), lambda b, meta: (0, b)),
            scratch_shapes=[pltpu.VMEM((deep, 4 * tokens), jnp.bfloat16)],
        ),
        out_shape=jax.ShapeDtypeStruct((deep, blocks * BLOCK), jnp.float32),
        compiler_params=params(),
    )(meta, places, *grads, *studs)


def build(sx, sz, sc):
    turn = lambda step: [
        (x * sx + y, ((y + step - x) % sx) * sx + y) for x in range(sx) for y in range(sx)
    ]
    spread_out = [(x * sx + y, y * sx + (x + y) % sx) for x in range(sx) for y in range(sx)]
    shift = lambda step: [(y, (y + step) % sx) for y in range(sx)]

    def to_owner(a, step):
        return lax.ppermute(a, ("x", "y"), turn(step))

    def both_cores(mine):
        if sc == 1:
            return mine[:, None]
        other = lax.ppermute(mine, "c", [(0, 1), (1, 0)])
        first = lax.axis_index("c") == 0
        return jnp.stack([jnp.where(first, mine, other), jnp.where(first, other, mine)], axis=1)

    def features(pay, tokens):
        full = both_cores(pay)
        chunks = full.shape[0] * full.shape[1]
        full = full.reshape(chunks, -1, BLOCK)
        teach = full[:, :tokens]
        stud = full[:, tokens:].reshape(chunks, tokens // BLOCK, -1, BLOCK)
        stud = stud.transpose(0, 2, 1, 3).reshape(-1, tokens)
        return teach, stud

    def neighbours(pay):
        after = lax.ppermute(pay, "y", shift(-1))
        before = lax.ppermute(pay, "y", shift(1))
        return after, before

    def opposite(pay):
        return lax.ppermute(pay, "y", shift(2))

    def everyone(stats):
        copies = jnp.broadcast_to(stats[None], (sx * sz * sc, *stats.shape))
        return lax.all_to_all(copies, LOCAL, split_axis=0, concat_axis=0, tiled=True)

    def dense(pays, head_t, head_s, allowed, target):
        tokens, blocks = allowed.shape
        width = head_t.shape[1]
        pairs = [features(pays[step], tokens) for step in range(sx)]
        teach = jnp.concatenate([t.transpose(1, 0, 2).reshape(tokens, -1) for t, _ in pairs])
        studs = jnp.concatenate([stud for _, stud in pairs], axis=1)
        part = jnp.concatenate(
            [dot(teach, head_t, ((1,), (0,))), dot(studs, head_s, ((0,), (0,)))], axis=1
        )
        total = sum(
            to_owner(part[step * tokens : (step + 1) * tokens], step) for step in range(sx)
        )
        lt, ls = total[:, :width], total[:, width:]
        open_ = jnp.broadcast_to((allowed > 0)[:, :, None], (tokens, blocks, BLOCK))
        open_ = open_.reshape(tokens, width)
        ids = jnp.arange(width, dtype=jnp.int32)
        picked = jnp.sum(jnp.where(ids[None, :] == target[:, None], ls, 0.0), axis=1)
        top_t = jnp.max(jnp.where(open_, lt, NEG), axis=1)
        top_s = jnp.max(jnp.where(open_, ls, NEG), axis=1)
        et = jnp.where(open_, jnp.exp(jnp.where(open_, lt, NEG) - top_t[:, None]), 0.0)
        es = jnp.where(open_, jnp.exp(jnp.where(open_, ls, NEG) - top_s[:, None]), 0.0)
        lines = [top_t, et.sum(1), (et * (lt - ls)).sum(1), top_s, es.sum(1), picked]
        stats = jnp.stack(lines + [jnp.zeros_like(top_t)] * 2)
        all_t, sum_t, all_s, sum_s, row_kl, logprob = combined(everyone(stats))
        scale_t = (jnp.exp(top_t[None] - all_t) / sum_t)[0]
        scale_s = (jnp.exp(top_s[None] - all_s) / sum_s)[0]
        grad = (es * scale_s[:, None] - et * scale_t[:, None]).astype(jnp.bfloat16)
        grads = jnp.concatenate([to_owner(grad, step) for step in range(sx)])
        head = dot(studs, grads, ((1,), (0,)))
        return row_kl[0], logprob[0], head

    def other_core(pay):
        return lax.ppermute(pay, "c", [(0, 1), (1, 0)]) if sc > 1 else pay

    def per_device(teacher_hidden, student_hidden, head_t, head_s, allowed, sampled):
        tokens, blocks = allowed.shape
        width = head_t.shape[1]
        stud = student_hidden.T.reshape(-1, tokens // BLOCK, BLOCK).transpose(1, 0, 2)
        pay = jnp.concatenate([teacher_hidden, stud.reshape(-1, BLOCK)], axis=0)
        pay = lax.ppermute(pay, ("x", "y"), spread_out)
        open_ = (allowed > 0).T.astype(jnp.float32)
        before = jnp.triu(jnp.ones((tokens, tokens), jnp.float32), 1)
        place = dot(open_.astype(jnp.bfloat16), before.astype(jnp.bfloat16), ((1,), (0,)))
        own_pos = jnp.where(open_ > 0, place.astype(jnp.int32), -1)
        own_pos = jnp.pad(own_pos, ((0, -blocks % 8), (0, 0)), constant_values=-1)
        order = (0, 1, 3, 2)

        def from_line(a, far):
            return lax.ppermute(a, "x", [(x, (x - far) % sx) for x in range(sx)])

        places = [own_pos] + [from_line(own_pos, far) for far in range(1, sx)]
        places = jnp.stack(places)
        pay = lax.all_to_all(jnp.broadcast_to(pay[None], (sz, *pay.shape)), "z", 0, 0, tiled=True)
        here, row, core = (lax.axis_index(name).astype(jnp.int32) for name in ("x", "y", "c"))
        meta = jnp.stack([core] + [(row + step - 2 * here) % sx for step in order])
        place_of = (row * sz + lax.axis_index("z")) * sc + core
        target = sampled - place_of * width

        def run(steps, mine, others):
            return partial_logits(meta, places, steps, mine, others, head_t, head_s)

        pay, other = lax.optimization_barrier((pay, other_core(pay)))
        after, ahead = neighbours(pay)
        part, stud0 = run((0,), [pay], [other])
        got = [to_owner(part, order[0])]
        far = opposite(pay)
        part, stud1 = run((1,), [after], [other_core(after)])
        got.append(to_owner(part, order[1]))
        part, stud3 = run((2,), [ahead], [other_core(ahead)])
        got.append(to_owner(part, order[2]))
        part, stud2 = run((3,), [far], [other_core(far)])
        got.append(to_owner(part, order[3]))

        early = early_sum(got[:3])
        logits, stats = row_stats(own_pos, target[None], places, early, got[3])
        grad, rows = row_grads(own_pos, everyone(stats), logits)
        grads = [grad] + [from_line(grad, far) for far in range(1, sx)]
        head = head_gradient(meta, places, grads, [stud0, stud1, stud3, stud2])
        start = (rows[2, 0] >= CAP, rows[0], rows[1], head)
        pays = {0: pay, 1: after, 3: ahead, 2: far}

        def redo(_):
            return (False, *dense(pays, head_t, head_s, allowed, target))

        return lax.while_loop(lambda held: held[0], redo, start)[1:]

    return per_device


def solution(mesh, sizes=(4, 8, 2)):
    sx, sz, sc = sizes
    grid = Mesh(mesh.devices.reshape(sx, sx, sz, sc), ("x", "y", "z", "c"))
    both = P("x", LOCAL)
    return jax.shard_map(
        build(sx, sz, sc),
        mesh=grid,
        in_specs=(both, both, both, both, both, P("x")),
        out_specs=(P("x"), P("x"), both),
        check_vma=False,
    )
```

```python
import functools

import jax
import jax.numpy as jnp
from jax import lax
from jax.experimental import pallas as pl
from jax.experimental.pallas import tpu as pltpu
from jax.sharding import Mesh
from jax.sharding import PartitionSpec as P

CAP = 80
LIST = 512
STARTS = 8
NEG = -1e30
BLOCK = 128
LOCAL = ("y", "z", "c")


def dot(a, b, dims):
    return lax.dot_general(a, b, (dims, ((), ())), preferred_element_type=jnp.float32)


def params(**kw):
    return pltpu.CompilerParams(vmem_limit_bytes=36 << 20, **kw)


def window(meta, held, b):
    run = meta[STARTS + held * 16 + b]
    start = pl.multiple_of(jnp.minimum(run, LIST - CAP), 16)
    return start, pl.ds(start, CAP), run - start


def selector(pos_row, start):
    lines = lax.broadcasted_iota(jnp.int32, (CAP, pos_row.shape[-1]), 0)
    return lines + start == pos_row


def from_row(first):
    return lax.broadcasted_iota(jnp.int32, (CAP, BLOCK), 0) >= first


def diagonal():
    rows = lax.broadcasted_iota(jnp.int32, (CAP, BLOCK), 0)
    return rows == lax.broadcasted_iota(jnp.int32, (CAP, BLOCK), 1)


def coded(logits):
    peak = jnp.max(jnp.abs(logits), axis=1, keepdims=True)
    power = jnp.floor(jnp.log2(jnp.maximum(peak, 1e-30)))
    scaled = jnp.round(logits * jnp.exp2(14.0 - power))
    values = jnp.clip(scaled, -32767.0, 32767.0).astype(jnp.int32)
    return values, jnp.sum(jnp.where(diagonal(), power, 0.0), axis=0, keepdims=True)


def decoded(values, powers):
    power = jnp.sum(jnp.where(diagonal(), powers, 0.0), axis=1, keepdims=True)
    return values.astype(jnp.int32).astype(jnp.float32) * jnp.exp2(power - 14.0)


def partial_kernel(steps, meta, pos, *refs):
    count = len(steps)
    mine, others = refs[:count], refs[count : 2 * count]
    far_t, far_s = refs[2 * count : 2 * count + 2]
    outs = refs[2 * count + 2 : 3 * count + 2]
    kept, sel, rows_t, rows_s, powers, head_t, head_s, sems = refs[3 * count + 2 :]
    fetch_t = pltpu.make_async_copy(far_t, head_t, sems.at[0])
    fetch_s = pltpu.make_async_copy(far_s, head_s, sems.at[1])
    fetch_t.start()
    fetch_s.start()
    blocks = far_t.shape[1] // BLOCK
    depth, tokens = mine[0].shape[0], sel.shape[1]
    both = kept.shape[1] // depth
    first = meta[0] == 0
    powers[...] = jnp.zeros_like(powers)
    for i in range(count):
        held = meta[1 + steps[i]]
        sel[...] = jnp.zeros_like(sel)
        for k in range(blocks):
            start, here, _ = window(meta, held, k)
            mark = selector(pos[held, k : k + 1, :], start).astype(jnp.float32)
            sel[here, :] = (sel[here, :].astype(jnp.float32) + mark).astype(jnp.bfloat16)

        def chunk(z, _, i=i):
            a, o = mine[i][z, :tokens, :], others[i][z, :tokens, :]
            pair = jnp.concatenate([jnp.where(first, a, o), jnp.where(first, o, a)], axis=1)
            rows_t[i, :, pl.ds(pl.multiple_of(z * 256, 256), 256)] = dot(
                sel[...], pair, ((1,), (0,))
            ).astype(jnp.bfloat16)
            a = mine[i][z, tokens:, :].astype(jnp.float32)
            o = others[i][z, tokens:, :].astype(jnp.float32)
            parts = []
            for part in (jnp.where(first, a, o), jnp.where(first, o, a)):
                parts.append(jnp.concatenate([part[: both // 2], part[both // 2 :]], axis=1))
            kept[i, pl.ds(pl.multiple_of(z * both, 16), both), :] = jnp.concatenate(
                parts, axis=0
            ).astype(jnp.bfloat16)
            return 0

        lax.fori_loop(0, depth, chunk, 0)
        deep_s = kept.shape[1]
        for at in range(0, deep_s, 256):
            end = min(at + 256, deep_s)
            rows_s[i, :, at:end] = dot(sel[...], kept[i, at:end, :], ((1,), (1,))).astype(
                jnp.bfloat16
            )

    def two_blocks(b, _):
        columns = pl.ds(pl.multiple_of(b * 2 * BLOCK, 2 * BLOCK), 2 * BLOCK)
        runs = [
            [window(meta, meta[1 + steps[i]], 2 * b + k) for k in range(2)] for i in range(count)
        ]
        for h, (rows, head) in enumerate(((rows_t, head_t), (rows_s, head_s))):
            lines = jnp.concatenate(
                [rows[i, runs[i][k][1], :] for i in range(count) for k in range(2)], axis=0
            )
            product = dot(lines, head[:, columns], ((1,), (0,)))
            for i in range(count):
                for k in range(2):
                    at = (2 * i + k) * CAP
                    values, power = coded(product[at : at + CAP, k * BLOCK : (k + 1) * BLOCK])
                    _, here, first = runs[i][k]
                    before = outs[i][0, h, here, :].astype(jnp.int32)
                    values = jnp.where(from_row(first), values, before)
                    outs[i][0, h, here, :] = values.astype(jnp.int16)
                    powers[2 * i + h, pl.ds(2 * b + k, 1), :] = power
        return 0

    fetch_t.wait()
    fetch_s.wait()
    lax.fori_loop(0, blocks // 2, two_blocks, 0)
    for i in range(count):
        for h in range(2):
            outs[i][0, h, LIST:, :] = powers[2 * i + h].astype(jnp.int32).astype(jnp.int16)


def partial_logits(meta, pos, steps, mine, others, head_t, head_s):
    count = len(steps)
    tokens = pos.shape[-1]
    deep_t, width = head_t.shape
    deep_s = head_s.shape[0]
    blocks = width // BLOCK
    coded_rows = LIST + 16
    return pl.pallas_call(
        functools.partial(partial_kernel, steps),
        name="partial_logits",
        in_specs=[pl.BlockSpec(memory_space=pltpu.SMEM)]
        + [pl.BlockSpec(memory_space=pltpu.VMEM)] * (2 * count + 1)
        + [pl.BlockSpec(memory_space=pl.ANY)] * 2,
        scratch_shapes=[
            pltpu.VMEM((LIST, tokens), jnp.bfloat16),
            pltpu.VMEM((count, LIST, deep_t), jnp.bfloat16),
            pltpu.VMEM((count, LIST, deep_s), jnp.bfloat16),
            pltpu.VMEM((2 * count, 16, BLOCK), jnp.float32),
            pltpu.VMEM(head_t.shape, head_t.dtype),
            pltpu.VMEM(head_s.shape, head_s.dtype),
            pltpu.SemaphoreType.DMA((2,)),
        ],
        out_shape=[jax.ShapeDtypeStruct((1, 2, coded_rows, BLOCK), jnp.int16)] * count
        + [jax.ShapeDtypeStruct((count, deep_s, tokens), jnp.bfloat16)],
        compiler_params=params(),
        cost_estimate=pl.CostEstimate(
            flops=8 * count * blocks * CAP * (deep_t + deep_s) * tokens,
            bytes_accessed=2 * (deep_t + deep_s) * (width + count * tokens),
            transcendentals=0,
        ),
    )(meta, pos, *mine, *others, head_t, head_s)


def spread(mark, line):
    return jnp.sum(jnp.where(mark, line, jnp.zeros_like(line)), axis=1, keepdims=True)


def fold(mark, column):
    return jnp.sum(jnp.where(mark, column, jnp.zeros_like(column)), axis=0, keepdims=True)


def unpacked(meta, ref, h, blocks):
    powers = ref[0, h, LIST:, :].astype(jnp.int32).astype(jnp.float32)
    return [
        decoded(ref[0, h, window(meta, 0, b)[1], :], powers[b : b + 1, :]) for b in range(blocks)
    ]


def early_kernel(meta, a0, a1, a2, total):
    blocks = total.shape[1]
    for h in range(2):
        parts = zip(*(unpacked(meta, a, h, blocks) for a in (a0, a1, a2)))
        for b, (x, y, z) in enumerate(parts):
            total[h, b] = x + y + z


def scalars_first(arrays):
    return [pl.BlockSpec(memory_space=pltpu.SMEM)] + [
        pl.BlockSpec(memory_space=pltpu.VMEM)
    ] * arrays


def early_sum(meta, blocks, parts):
    return pl.pallas_call(
        early_kernel,
        name="early_sum",
        in_specs=scalars_first(3),
        out_shape=jax.ShapeDtypeStruct((2, blocks, CAP, BLOCK), jnp.float32),
        compiler_params=params(),
    )(meta, *parts)


def stats_kernel(meta, pos, target, places, early, last, logits, stats):
    blocks = logits.shape[1]
    tokens = pos.shape[-1]
    tops = [jnp.full((1, tokens), NEG, jnp.float32) for _ in range(2)]
    for h in range(2):
        for b, part in enumerate(unpacked(meta, last, h, blocks)):
            total = early[h, b] + part
            logits[h, b] = total
            peak = jnp.max(total, axis=1, keepdims=True)
            mark = selector(pos[b : b + 1, :], window(meta, 0, b)[0])
            tops[h] = jnp.maximum(
                tops[h], jnp.max(jnp.where(mark, peak, NEG), axis=0, keepdims=True)
            )
    zero = jnp.zeros((1, tokens), jnp.float32)
    sum_t, cross, sum_s, picked = zero, zero, zero, zero
    lanes = lax.broadcasted_iota(jnp.int32, (CAP, BLOCK), 1)
    for b in range(blocks):
        mark = selector(pos[b : b + 1, :], window(meta, 0, b)[0])
        lt, ls = logits[0, b], logits[1, b]
        et = jnp.exp(lt - spread(mark, tops[0]))
        es = jnp.exp(ls - spread(mark, tops[1]))
        wanted = spread(mark, target[...] - b * BLOCK)
        sum_t = sum_t + fold(mark, jnp.sum(et, axis=1, keepdims=True))
        cross = cross + fold(mark, jnp.sum(et * (lt - ls), axis=1, keepdims=True))
        sum_s = sum_s + fold(mark, jnp.sum(es, axis=1, keepdims=True))
        picked = picked + fold(
            mark, jnp.sum(jnp.where(lanes == wanted, ls, 0.0), axis=1, keepdims=True)
        )
    most = jnp.max(jnp.concatenate([places[t, 11:12, :] for t in range(4)]), axis=0, keepdims=True)
    most = most.astype(jnp.float32)
    lines = [tops[0], sum_t, cross, tops[1], sum_s, picked, most, zero]
    stats[...] = jnp.concatenate(lines, axis=0)


def row_stats(meta, pos, target, places, early, last):
    return pl.pallas_call(
        stats_kernel,
        name="row_stats",
        in_specs=scalars_first(5),
        out_shape=[
            jax.ShapeDtypeStruct(early.shape, jnp.float32),
            jax.ShapeDtypeStruct((8, pos.shape[-1]), jnp.float32),
        ],
        compiler_params=params(),
    )(meta, pos, target, places, early, last)


def combined(seen):
    top_t = jnp.max(seen[:, 0, :], axis=0, keepdims=True)
    top_s = jnp.max(seen[:, 3, :], axis=0, keepdims=True)
    scale_t = jnp.exp(seen[:, 0, :] - top_t)
    scale_s = jnp.exp(seen[:, 3, :] - top_s)
    total = lambda a: jnp.sum(a, axis=0, keepdims=True)
    sum_t = total(seen[:, 1, :] * scale_t)
    cross = total(seen[:, 2, :] * scale_t)
    sum_s = total(seen[:, 4, :] * scale_s)
    picked = total(seen[:, 5, :])
    log_t = top_t + jnp.log(sum_t)
    log_s = top_s + jnp.log(sum_s)
    return top_t, sum_t, top_s, sum_s, cross / sum_t - log_t + log_s, picked - log_s


def grad_kernel(meta, pos, seen, logits, grad, rows, lines):
    top_t, sum_t, top_s, sum_s, row_kl, logprob = combined(seen[...])
    most = jnp.max(seen[:, 6, :], axis=0, keepdims=True)
    rows[...] = jnp.concatenate([row_kl, logprob, most] + [most] * 5, axis=0)
    inv_t, inv_s = 1.0 / sum_t, 1.0 / sum_s
    lines[...] = jnp.zeros_like(lines)
    for b in range(logits.shape[1]):
        start, here, first = window(meta, 0, b)
        mark = selector(pos[b : b + 1, :], start)
        share_t, share_s = spread(mark, inv_t), spread(mark, inv_s)
        et = jnp.exp(logits[0, b] - spread(mark, top_t)) * share_t
        es = jnp.exp(logits[1, b] - spread(mark, top_s)) * share_s
        own = jnp.where(share_s > 0.0, es - et, 0.0)
        lines[here, :] = jnp.where(from_row(first), own, lines[here, :])
    grad[...] = lines[...].astype(jnp.bfloat16)


def row_grads(meta, pos, seen, logits):
    return pl.pallas_call(
        grad_kernel,
        name="row_grads",
        in_specs=scalars_first(3),
        out_shape=[
            jax.ShapeDtypeStruct((LIST, BLOCK), jnp.bfloat16),
            jax.ShapeDtypeStruct((8, pos.shape[-1]), jnp.float32),
        ],
        scratch_shapes=[pltpu.VMEM((LIST, BLOCK), jnp.float32)],
        compiler_params=params(),
    )(meta, pos, seen, logits)


def head_kernel(meta, places, *refs):
    *studs, out, left = refs
    grads, studs = studs[:4], studs[4:]
    tokens = places.shape[-1]
    b = pl.program_id(0)

    @pl.when(b == 0)
    def _():
        step = 1
        for ref in studs:
            for i in range(ref.shape[0]):
                at = pl.multiple_of(meta[step] * tokens, tokens)
                left[:, pl.ds(at, tokens)] = ref[i]
                step += 1

    right = []
    for t, grad in enumerate(grads):
        pair = []
        for k in range(2):
            start, here, _ = window(meta, t, 2 * b + k)
            mark = selector(places[t, 2 * b + k][None], start).astype(jnp.float32)
            mark = mark.astype(jnp.bfloat16)
            pair.append(dot(mark, grad[here, :], ((0,), (0,))).astype(jnp.bfloat16))
        right.append(jnp.concatenate(pair, axis=1))
    out[...] = dot(left[...], jnp.concatenate(right, axis=0), ((1,), (0,)))


def head_gradient(meta, places, grads, studs, blocks):
    deep, tokens = studs[0].shape[1:]
    whole = lambda a: pl.BlockSpec(a.shape, lambda b, meta: (0,) * a.ndim)
    return pl.pallas_call(
        head_kernel,
        name="head_gradient",
        grid_spec=pltpu.PrefetchScalarGridSpec(
            num_scalar_prefetch=1,
            grid=(blocks // 2,),
            in_specs=[whole(places)]
            + [whole(a) for a in (*grads, *studs)],
            out_specs=pl.BlockSpec((deep, 2 * BLOCK), lambda b, meta: (0, b)),
            scratch_shapes=[pltpu.VMEM((deep, 4 * tokens), jnp.bfloat16)],
        ),
        out_shape=jax.ShapeDtypeStruct((deep, blocks * BLOCK), jnp.float32),
        compiler_params=params(),
    )(meta, places, *grads, *studs)


def build(sx, sz, sc):
    turn = lambda step: [
        (x * sx + y, ((y + step - x) % sx) * sx + y) for x in range(sx) for y in range(sx)
    ]
    spread_out = [(x * sx + y, y * sx + (x + y) % sx) for x in range(sx) for y in range(sx)]
    shift = lambda step: [(y, (y + step) % sx) for y in range(sx)]

    def to_owner(a, step):
        return lax.ppermute(a, ("x", "y"), turn(step))

    def both_cores(mine):
        if sc == 1:
            return mine[:, None]
        other = lax.ppermute(mine, "c", [(0, 1), (1, 0)])
        first = lax.axis_index("c") == 0
        return jnp.stack([jnp.where(first, mine, other), jnp.where(first, other, mine)], axis=1)

    def features(pay, tokens):
        full = both_cores(pay)
        chunks = full.shape[0] * full.shape[1]
        full = full.reshape(chunks, -1, BLOCK)
        teach = full[:, :tokens]
        stud = full[:, tokens:].reshape(chunks, tokens // BLOCK, -1, BLOCK)
        stud = stud.transpose(0, 2, 1, 3).reshape(-1, tokens)
        return teach, stud

    def neighbours(pay):
        after = lax.ppermute(pay, "y", shift(-1))
        before = lax.ppermute(pay, "y", shift(1))
        return after, before

    def opposite(pay):
        return lax.ppermute(pay, "y", shift(2))

    def everyone(stats):
        copies = jnp.broadcast_to(stats[None], (sx * sz * sc, *stats.shape))
        return lax.all_to_all(copies, LOCAL, split_axis=0, concat_axis=0, tiled=True)

    def dense(pays, head_t, head_s, allowed, target):
        tokens, blocks = allowed.shape
        width = head_t.shape[1]
        pairs = [features(pays[step], tokens) for step in range(sx)]
        teach = jnp.concatenate([t.transpose(1, 0, 2).reshape(tokens, -1) for t, _ in pairs])
        studs = jnp.concatenate([stud for _, stud in pairs], axis=1)
        part = jnp.concatenate(
            [dot(teach, head_t, ((1,), (0,))), dot(studs, head_s, ((0,), (0,)))], axis=1
        )
        total = sum(
            to_owner(part[step * tokens : (step + 1) * tokens], step) for step in range(sx)
        )
        lt, ls = total[:, :width], total[:, width:]
        open_ = jnp.broadcast_to((allowed > 0)[:, :, None], (tokens, blocks, BLOCK))
        open_ = open_.reshape(tokens, width)
        ids = jnp.arange(width, dtype=jnp.int32)
        picked = jnp.sum(jnp.where(ids[None, :] == target[:, None], ls, 0.0), axis=1)
        top_t = jnp.max(jnp.where(open_, lt, NEG), axis=1)
        top_s = jnp.max(jnp.where(open_, ls, NEG), axis=1)
        et = jnp.where(open_, jnp.exp(jnp.where(open_, lt, NEG) - top_t[:, None]), 0.0)
        es = jnp.where(open_, jnp.exp(jnp.where(open_, ls, NEG) - top_s[:, None]), 0.0)
        lines = [top_t, et.sum(1), (et * (lt - ls)).sum(1), top_s, es.sum(1), picked]
        stats = jnp.stack(lines + [jnp.zeros_like(top_t)] * 2)
        all_t, sum_t, all_s, sum_s, row_kl, logprob = combined(everyone(stats))
        scale_t = (jnp.exp(top_t[None] - all_t) / sum_t)[0]
        scale_s = (jnp.exp(top_s[None] - all_s) / sum_s)[0]
        grad = (es * scale_s[:, None] - et * scale_t[:, None]).astype(jnp.bfloat16)
        grads = jnp.concatenate([to_owner(grad, step) for step in range(sx)])
        head = dot(studs, grads, ((1,), (0,)))
        return row_kl[0], logprob[0], head

    def other_core(pay):
        return lax.ppermute(pay, "c", [(0, 1), (1, 0)]) if sc > 1 else pay

    def per_device(teacher_hidden, student_hidden, head_t, head_s, allowed, sampled):
        tokens, blocks = allowed.shape
        width = head_t.shape[1]
        stud = student_hidden.T.reshape(-1, tokens // BLOCK, BLOCK).transpose(1, 0, 2)
        pay = jnp.concatenate([teacher_hidden, stud.reshape(-1, BLOCK)], axis=0)
        pay = lax.ppermute(pay, ("x", "y"), spread_out)
        open_ = (allowed > 0).T.astype(jnp.float32)
        before = jnp.triu(jnp.ones((tokens, tokens), jnp.float32), 1)
        place = dot(open_.astype(jnp.bfloat16), before.astype(jnp.bfloat16), ((1,), (0,)))
        count = jnp.sum(open_, axis=1).astype(jnp.int32)
        room = (count + 15) // 16 * 16
        ahead_of = jnp.arange(blocks)[None, :] < jnp.arange(blocks)[:, None]
        runs = jnp.sum(jnp.where(ahead_of, room[None, :], 0), axis=1)
        over = jnp.logical_or(jnp.sum(room) > LIST, jnp.max(count) > CAP).astype(jnp.int32)
        own_pos = jnp.where(open_ > 0, place.astype(jnp.int32) + runs[:, None], -1)
        own_pos = jnp.concatenate(
            [
                own_pos,
                jnp.pad(jnp.minimum(runs, LIST), (0, tokens - blocks))[None],
                jnp.broadcast_to(over, (6 - blocks % 8 + 1, tokens)),
            ]
        )
        order = (0, 1, 3, 2)

        def from_line(a, far):
            return lax.ppermute(a, "x", [(x, (x - far) % sx) for x in range(sx)])

        places = [own_pos] + [from_line(own_pos, far) for far in range(1, sx)]
        places = jnp.stack(places)
        pay = lax.all_to_all(jnp.broadcast_to(pay[None], (sz, *pay.shape)), "z", 0, 0, tiled=True)
        here, row, core = (lax.axis_index(name).astype(jnp.int32) for name in ("x", "y", "c"))
        meta = jnp.stack([core] + [(row + step - 2 * here) % sx for step in order] + [core] * 3)
        meta = jnp.concatenate([meta, places[:, blocks, :16].reshape(-1)])
        place_of = (row * sz + lax.axis_index("z")) * sc + core
        target = sampled - place_of * width

        def run(steps, mine, others):
            return partial_logits(meta, places, steps, mine, others, head_t, head_s)

        pay, other = lax.optimization_barrier((pay, other_core(pay)))
        after, ahead = neighbours(pay)
        part, stud0 = run((0,), [pay], [other])
        got = [to_owner(part, order[0])]
        far = opposite(pay)
        part, stud1 = run((1,), [after], [other_core(after)])
        got.append(to_owner(part, order[1]))
        part, stud3 = run((2,), [ahead], [other_core(ahead)])
        got.append(to_owner(part, order[2]))
        part, stud2 = run((3,), [far], [other_core(far)])
        got.append(to_owner(part, order[3]))

        early = early_sum(meta, blocks, got[:3])
        logits, stats = row_stats(meta, own_pos, target[None], places, early, got[3])
        grad, rows = row_grads(meta, own_pos, everyone(stats), logits)
        grads = [grad] + [from_line(grad, far) for far in range(1, sx)]
        head = head_gradient(meta, places, grads, [stud0, stud1, stud3, stud2], blocks)
        start = (rows[2, 0] > 0.5, rows[0], rows[1], head)
        pays = {0: pay, 1: after, 3: ahead, 2: far}

        def redo(_):
            return (False, *dense(pays, head_t, head_s, allowed, target))

        return lax.while_loop(lambda held: held[0], redo, start)[1:]

    return per_device


def solution(mesh, sizes=(4, 8, 2)):
    sx, sz, sc = sizes
    grid = Mesh(mesh.devices.reshape(sx, sx, sz, sc), ("x", "y", "z", "c"))
    both = P("x", LOCAL)
    return jax.shard_map(
        build(sx, sz, sc),
        mesh=grid,
        in_specs=(both, both, both, both, both, P("x")),
        out_specs=(P("x"), P("x"), both),
        check_vma=False,
    )
```

```python
import functools

import jax
import jax.numpy as jnp
from jax import lax
from jax.experimental import pallas as pl
from jax.experimental.pallas import tpu as pltpu
from jax.sharding import Mesh
from jax.sharding import PartitionSpec as P

CAP = 80
LIST = 512
STARTS = 8
NEG = -1e30
OVER = 1e30
BLOCK = 128
LOCAL = ("y", "z", "c")


def dot(a, b, dims):
    return lax.dot_general(a, b, (dims, ((), ())), preferred_element_type=jnp.float32)


def params(**kw):
    return pltpu.CompilerParams(vmem_limit_bytes=36 << 20, **kw)


def window(meta, held, b):
    run = meta[STARTS + held * 16 + b]
    start = pl.multiple_of(jnp.minimum(run, LIST - CAP), 16)
    return start, pl.ds(start, CAP), run - start


def selector(pos_row, start):
    lines = lax.broadcasted_iota(jnp.int32, (CAP, pos_row.shape[-1]), 0)
    return lines + start == pos_row


def from_row(first):
    return lax.broadcasted_iota(jnp.int32, (CAP, BLOCK), 0) >= first


def diagonal():
    rows = lax.broadcasted_iota(jnp.int32, (CAP, BLOCK), 0)
    return rows == lax.broadcasted_iota(jnp.int32, (CAP, BLOCK), 1)


def coded(logits):
    peak = jnp.max(jnp.abs(logits), axis=1, keepdims=True)
    power = jnp.floor(jnp.log2(jnp.maximum(peak, 1e-30)))
    scaled = jnp.round(logits * jnp.exp2(14.0 - power))
    values = jnp.clip(scaled, -32767.0, 32767.0).astype(jnp.int32)
    return values, jnp.sum(jnp.where(diagonal(), power, 0.0), axis=0, keepdims=True)


def decoded(values, powers):
    power = jnp.sum(jnp.where(diagonal(), powers, 0.0), axis=1, keepdims=True)
    return values.astype(jnp.int32).astype(jnp.float32) * jnp.exp2(power - 14.0)


def partial_kernel(steps, meta, pos, *refs):
    count = len(steps)
    mine, others = refs[:count], refs[count : 2 * count]
    far_t, far_s = refs[2 * count : 2 * count + 2]
    outs = refs[2 * count + 2 : 3 * count + 2]
    kept, sel, rows_t, rows_s, powers, head_t, head_s, sems = refs[3 * count + 2 :]
    fetch_t = pltpu.make_async_copy(far_t, head_t, sems.at[0])
    fetch_s = pltpu.make_async_copy(far_s, head_s, sems.at[1])
    fetch_t.start()
    fetch_s.start()
    blocks = far_t.shape[1] // BLOCK
    depth, tokens = mine[0].shape[0], sel.shape[1]
    both = kept.shape[1] // depth
    first = meta[0] == 0
    powers[...] = jnp.zeros_like(powers)
    for i in range(count):
        held = meta[1 + steps[i]]
        sel[...] = jnp.zeros_like(sel)
        for k in range(blocks):
            start, here, _ = window(meta, held, k)
            mark = selector(pos[held, k : k + 1, :], start).astype(jnp.float32)
            sel[here, :] = (sel[here, :].astype(jnp.float32) + mark).astype(jnp.bfloat16)

        def chunk(z, _, i=i):
            a, o = mine[i][z, :tokens, :], others[i][z, :tokens, :]
            pair = jnp.concatenate([jnp.where(first, a, o), jnp.where(first, o, a)], axis=1)
            rows_t[i, :, pl.ds(pl.multiple_of(z * 256, 256), 256)] = dot(
                sel[...], pair, ((1,), (0,))
            ).astype(jnp.bfloat16)
            a = mine[i][z, tokens:, :].astype(jnp.float32)
            o = others[i][z, tokens:, :].astype(jnp.float32)
            parts = []
            for part in (jnp.where(first, a, o), jnp.where(first, o, a)):
                parts.append(jnp.concatenate([part[: both // 2], part[both // 2 :]], axis=1))
            kept[i, pl.ds(pl.multiple_of(z * both, 16), both), :] = jnp.concatenate(
                parts, axis=0
            ).astype(jnp.bfloat16)
            return 0

        lax.fori_loop(0, depth, chunk, 0)
        deep_s = kept.shape[1]
        for at in range(0, deep_s, 256):
            end = min(at + 256, deep_s)
            rows_s[i, :, at:end] = dot(sel[...], kept[i, at:end, :], ((1,), (1,))).astype(
                jnp.bfloat16
            )

    def two_blocks(b, _):
        columns = pl.ds(pl.multiple_of(b * 2 * BLOCK, 2 * BLOCK), 2 * BLOCK)
        runs = [
            [window(meta, meta[1 + steps[i]], 2 * b + k) for k in range(2)] for i in range(count)
        ]
        for h, (rows, head) in enumerate(((rows_t, head_t), (rows_s, head_s))):
            lines = jnp.concatenate(
                [rows[i, runs[i][k][1], :] for i in range(count) for k in range(2)], axis=0
            )
            product = dot(lines, head[:, columns], ((1,), (0,)))
            for i in range(count):
                for k in range(2):
                    at = (2 * i + k) * CAP
                    values, power = coded(product[at : at + CAP, k * BLOCK : (k + 1) * BLOCK])
                    _, here, first = runs[i][k]
                    before = outs[i][0, h, here, :].astype(jnp.int32)
                    values = jnp.where(from_row(first), values, before)
                    outs[i][0, h, here, :] = values.astype(jnp.int16)
                    powers[2 * i + h, pl.ds(2 * b + k, 1), :] = power
        return 0

    fetch_t.wait()
    fetch_s.wait()
    lax.fori_loop(0, blocks // 2, two_blocks, 0)
    for i in range(count):
        for h in range(2):
            outs[i][0, h, LIST:, :] = powers[2 * i + h].astype(jnp.int32).astype(jnp.int16)


def partial_logits(meta, pos, steps, mine, others, head_t, head_s):
    count = len(steps)
    tokens = pos.shape[-1]
    deep_t, width = head_t.shape
    deep_s = head_s.shape[0]
    blocks = width // BLOCK
    coded_rows = LIST + 16
    return pl.pallas_call(
        functools.partial(partial_kernel, steps),
        name="partial_logits",
        in_specs=[pl.BlockSpec(memory_space=pltpu.SMEM)]
        + [pl.BlockSpec(memory_space=pltpu.VMEM)] * (2 * count + 1)
        + [pl.BlockSpec(memory_space=pl.ANY)] * 2,
        scratch_shapes=[
            pltpu.VMEM((LIST, tokens), jnp.bfloat16),
            pltpu.VMEM((count, LIST, deep_t), jnp.bfloat16),
            pltpu.VMEM((count, LIST, deep_s), jnp.bfloat16),
            pltpu.VMEM((2 * count, 16, BLOCK), jnp.float32),
            pltpu.VMEM(head_t.shape, head_t.dtype),
            pltpu.VMEM(head_s.shape, head_s.dtype),
            pltpu.SemaphoreType.DMA((2,)),
        ],
        out_shape=[jax.ShapeDtypeStruct((1, 2, coded_rows, BLOCK), jnp.int16)] * count
        + [jax.ShapeDtypeStruct((count, deep_s, tokens), jnp.bfloat16)],
        compiler_params=params(),
        cost_estimate=pl.CostEstimate(
            flops=8 * count * blocks * CAP * (deep_t + deep_s) * tokens,
            bytes_accessed=2 * (deep_t + deep_s) * (width + count * tokens),
            transcendentals=0,
        ),
    )(meta, pos, *mine, *others, head_t, head_s)


def spread(mark, line):
    return jnp.sum(jnp.where(mark, line, jnp.zeros_like(line)), axis=1, keepdims=True)


def fold(mark, column):
    return jnp.sum(jnp.where(mark, column, jnp.zeros_like(column)), axis=0, keepdims=True)


def unpacked(meta, ref, h, blocks):
    powers = ref[0, h, LIST:, :].astype(jnp.int32).astype(jnp.float32)
    return [
        decoded(ref[0, h, window(meta, 0, b)[1], :], powers[b : b + 1, :]) for b in range(blocks)
    ]


def early_kernel(meta, a0, a1, a2, total):
    blocks = total.shape[1]
    for h in range(2):
        parts = zip(*(unpacked(meta, a, h, blocks) for a in (a0, a1, a2)))
        for b, (x, y, z) in enumerate(parts):
            total[h, b] = x + y + z


def scalars_first(arrays):
    return [pl.BlockSpec(memory_space=pltpu.SMEM)] + [
        pl.BlockSpec(memory_space=pltpu.VMEM)
    ] * arrays


def early_sum(meta, blocks, parts):
    return pl.pallas_call(
        early_kernel,
        name="early_sum",
        in_specs=scalars_first(3),
        out_shape=jax.ShapeDtypeStruct((2, blocks, CAP, BLOCK), jnp.float32),
        compiler_params=params(),
    )(meta, *parts)


def packed(top_t, sum_t, cross, top_s, sum_s, picked, over):
    some = sum_t > 0.0
    safe_t, safe_s = jnp.where(some, sum_t, 1.0), jnp.where(some, sum_s, 1.0)
    lse_t = jnp.where(some, top_t + jnp.log(safe_t), NEG)
    lse_s = jnp.where(some, top_s + jnp.log(safe_s), NEG)
    lines = [jnp.where(over, OVER, lse_t), jnp.where(some, cross / safe_t, 0.0), lse_s, picked]
    half = picked.shape[-1] // 2
    return jnp.concatenate([part for a in lines for part in (a[:, :half], a[:, half:])], axis=0)


def stats_kernel(meta, pos, target, places, early, last, logits, stats):
    blocks = logits.shape[1]
    tokens = pos.shape[-1]
    tops = [jnp.full((1, tokens), NEG, jnp.float32) for _ in range(2)]
    for h in range(2):
        for b, part in enumerate(unpacked(meta, last, h, blocks)):
            total = early[h, b] + part
            logits[h, b] = total
            peak = jnp.max(total, axis=1, keepdims=True)
            mark = selector(pos[b : b + 1, :], window(meta, 0, b)[0])
            tops[h] = jnp.maximum(
                tops[h], jnp.max(jnp.where(mark, peak, NEG), axis=0, keepdims=True)
            )
    zero = jnp.zeros((1, tokens), jnp.float32)
    sum_t, cross, sum_s, picked = zero, zero, zero, zero
    lanes = lax.broadcasted_iota(jnp.int32, (CAP, BLOCK), 1)
    for b in range(blocks):
        mark = selector(pos[b : b + 1, :], window(meta, 0, b)[0])
        lt, ls = logits[0, b], logits[1, b]
        et = jnp.exp(lt - spread(mark, tops[0]))
        es = jnp.exp(ls - spread(mark, tops[1]))
        wanted = spread(mark, target[...] - b * BLOCK)
        sum_t = sum_t + fold(mark, jnp.sum(et, axis=1, keepdims=True))
        cross = cross + fold(mark, jnp.sum(et * (lt - ls), axis=1, keepdims=True))
        sum_s = sum_s + fold(mark, jnp.sum(es, axis=1, keepdims=True))
        picked = picked + fold(
            mark, jnp.sum(jnp.where(lanes == wanted, ls, 0.0), axis=1, keepdims=True)
        )
    over = jnp.max(jnp.concatenate([places[t, 11:12, :] for t in range(4)]), axis=0, keepdims=True)
    stats[...] = packed(tops[0], sum_t, cross, tops[1], sum_s, picked, over > 0)


def row_stats(meta, pos, target, places, early, last):
    return pl.pallas_call(
        stats_kernel,
        name="row_stats",
        in_specs=scalars_first(5),
        out_shape=[
            jax.ShapeDtypeStruct(early.shape, jnp.float32),
            jax.ShapeDtypeStruct((8, pos.shape[-1] // 2), jnp.float32),
        ],
        compiler_params=params(),
    )(meta, pos, target, places, early, last)


def combined(seen):
    lse_t, ratio, lse_s, picked = (
        jnp.concatenate([seen[:, 2 * k, :], seen[:, 2 * k + 1, :]], axis=1) for k in range(4)
    )
    total = lambda a: jnp.sum(a, axis=0, keepdims=True)
    top_t = jnp.max(lse_t, axis=0, keepdims=True)
    top_s = jnp.max(lse_s, axis=0, keepdims=True)
    share_t = jnp.exp(lse_t - top_t)
    sum_t = total(share_t)
    log_t = top_t + jnp.log(sum_t)
    log_s = top_s + jnp.log(total(jnp.exp(lse_s - top_s)))
    row_kl = total(share_t * ratio) / sum_t - log_t + log_s
    return log_t, log_s, row_kl, total(picked) - log_s, top_t


def grad_kernel(meta, pos, seen, logits, grad, rows, lines):
    log_t, log_s, row_kl, logprob, top = combined(seen[...])
    rows[...] = jnp.concatenate([row_kl, logprob, top] + [top] * 5, axis=0)
    lines[...] = jnp.zeros_like(lines)
    for b in range(logits.shape[1]):
        start, here, first = window(meta, 0, b)
        mark = selector(pos[b : b + 1, :], start)
        et = jnp.exp(logits[0, b] - spread(mark, log_t))
        es = jnp.exp(logits[1, b] - spread(mark, log_s))
        own = jnp.where(spread(mark, jnp.ones_like(log_t)) > 0.0, es - et, 0.0)
        lines[here, :] = jnp.where(from_row(first), own, lines[here, :])
    grad[...] = lines[...].astype(jnp.bfloat16)


def row_grads(meta, pos, seen, logits):
    return pl.pallas_call(
        grad_kernel,
        name="row_grads",
        in_specs=scalars_first(3),
        out_shape=[
            jax.ShapeDtypeStruct((LIST, BLOCK), jnp.bfloat16),
            jax.ShapeDtypeStruct((8, pos.shape[-1]), jnp.float32),
        ],
        scratch_shapes=[pltpu.VMEM((LIST, BLOCK), jnp.float32)],
        compiler_params=params(),
    )(meta, pos, seen, logits)


def head_kernel(meta, places, *refs):
    *studs, out, left = refs
    grads, studs = studs[:4], studs[4:]
    tokens = places.shape[-1]
    b = pl.program_id(0)

    @pl.when(b == 0)
    def _():
        step = 1
        for ref in studs:
            for i in range(ref.shape[0]):
                at = pl.multiple_of(meta[step] * tokens, tokens)
                left[:, pl.ds(at, tokens)] = ref[i]
                step += 1

    right = []
    for t, grad in enumerate(grads):
        pair = []
        for k in range(2):
            start, here, _ = window(meta, t, 2 * b + k)
            mark = selector(places[t, 2 * b + k][None], start).astype(jnp.float32)
            mark = mark.astype(jnp.bfloat16)
            pair.append(dot(mark, grad[here, :], ((0,), (0,))).astype(jnp.bfloat16))
        right.append(jnp.concatenate(pair, axis=1))
    out[...] = dot(left[...], jnp.concatenate(right, axis=0), ((1,), (0,)))


def head_gradient(meta, places, grads, studs, blocks):
    deep, tokens = studs[0].shape[1:]
    whole = lambda a: pl.BlockSpec(a.shape, lambda b, meta: (0,) * a.ndim)
    return pl.pallas_call(
        head_kernel,
        name="head_gradient",
        grid_spec=pltpu.PrefetchScalarGridSpec(
            num_scalar_prefetch=1,
            grid=(blocks // 2,),
            in_specs=[whole(places)]
            + [whole(a) for a in (*grads, *studs)],
            out_specs=pl.BlockSpec((deep, 2 * BLOCK), lambda b, meta: (0, b)),
            scratch_shapes=[pltpu.VMEM((deep, 4 * tokens), jnp.bfloat16)],
        ),
        out_shape=jax.ShapeDtypeStruct((deep, blocks * BLOCK), jnp.float32),
        compiler_params=params(),
    )(meta, places, *grads, *studs)


def build(sx, sz, sc):
    turn = lambda step: [
        (x * sx + y, ((y + step - x) % sx) * sx + y) for x in range(sx) for y in range(sx)
    ]
    spread_out = [(x * sx + y, y * sx + (x + y) % sx) for x in range(sx) for y in range(sx)]
    shift = lambda step: [(y, (y + step) % sx) for y in range(sx)]

    def to_owner(a, step):
        return lax.ppermute(a, ("x", "y"), turn(step))

    def both_cores(mine):
        if sc == 1:
            return mine[:, None]
        other = lax.ppermute(mine, "c", [(0, 1), (1, 0)])
        first = lax.axis_index("c") == 0
        return jnp.stack([jnp.where(first, mine, other), jnp.where(first, other, mine)], axis=1)

    def features(pay, tokens):
        full = both_cores(pay)
        chunks = full.shape[0] * full.shape[1]
        full = full.reshape(chunks, -1, BLOCK)
        teach = full[:, :tokens]
        stud = full[:, tokens:].reshape(chunks, tokens // BLOCK, -1, BLOCK)
        stud = stud.transpose(0, 2, 1, 3).reshape(-1, tokens)
        return teach, stud

    def neighbours(pay):
        after = lax.ppermute(pay, "y", shift(-1))
        before = lax.ppermute(pay, "y", shift(1))
        return after, before

    def opposite(pay):
        return lax.ppermute(pay, "y", shift(2))

    def everyone(stats):
        copies = jnp.broadcast_to(stats[None], (sx * sz * sc, *stats.shape))
        return lax.all_to_all(copies, LOCAL, split_axis=0, concat_axis=0, tiled=True)

    def dense(pays, head_t, head_s, allowed, target):
        tokens, blocks = allowed.shape
        width = head_t.shape[1]
        pairs = [features(pays[step], tokens) for step in range(sx)]
        teach = jnp.concatenate([t.transpose(1, 0, 2).reshape(tokens, -1) for t, _ in pairs])
        studs = jnp.concatenate([stud for _, stud in pairs], axis=1)
        part = jnp.concatenate(
            [dot(teach, head_t, ((1,), (0,))), dot(studs, head_s, ((0,), (0,)))], axis=1
        )
        total = sum(
            to_owner(part[step * tokens : (step + 1) * tokens], step) for step in range(sx)
        )
        lt, ls = total[:, :width], total[:, width:]
        open_ = jnp.broadcast_to((allowed > 0)[:, :, None], (tokens, blocks, BLOCK))
        open_ = open_.reshape(tokens, width)
        ids = jnp.arange(width, dtype=jnp.int32)
        picked = jnp.sum(jnp.where(ids[None, :] == target[:, None], ls, 0.0), axis=1)
        top_t = jnp.max(jnp.where(open_, lt, NEG), axis=1)
        top_s = jnp.max(jnp.where(open_, ls, NEG), axis=1)
        et = jnp.where(open_, jnp.exp(jnp.where(open_, lt, NEG) - top_t[:, None]), 0.0)
        es = jnp.where(open_, jnp.exp(jnp.where(open_, ls, NEG) - top_s[:, None]), 0.0)
        lines = [top_t, et.sum(1), (et * (lt - ls)).sum(1), top_s, es.sum(1), picked]
        stats = packed(*(line[None] for line in lines), False)
        log_t, log_s, row_kl, logprob, _ = combined(everyone(stats))
        scale_t = jnp.exp(top_t - log_t[0])
        scale_s = jnp.exp(top_s - log_s[0])
        grad = (es * scale_s[:, None] - et * scale_t[:, None]).astype(jnp.bfloat16)
        grads = jnp.concatenate([to_owner(grad, step) for step in range(sx)])
        head = dot(studs, grads, ((1,), (0,)))
        return row_kl[0], logprob[0], head

    def other_core(pay):
        return lax.ppermute(pay, "c", [(0, 1), (1, 0)]) if sc > 1 else pay

    def per_device(teacher_hidden, student_hidden, head_t, head_s, allowed, sampled):
        tokens, blocks = allowed.shape
        width = head_t.shape[1]
        stud = student_hidden.T.reshape(-1, tokens // BLOCK, BLOCK).transpose(1, 0, 2)
        pay = jnp.concatenate([teacher_hidden, stud.reshape(-1, BLOCK)], axis=0)
        pay = lax.ppermute(pay, ("x", "y"), spread_out)
        open_ = (allowed > 0).T.astype(jnp.float32)
        before = jnp.triu(jnp.ones((tokens, tokens), jnp.float32), 1)
        place = dot(open_.astype(jnp.bfloat16), before.astype(jnp.bfloat16), ((1,), (0,)))
        count = jnp.sum(open_, axis=1).astype(jnp.int32)
        room = (count + 15) // 16 * 16
        ahead_of = jnp.arange(blocks)[None, :] < jnp.arange(blocks)[:, None]
        runs = jnp.sum(jnp.where(ahead_of, room[None, :], 0), axis=1)
        over = jnp.logical_or(jnp.sum(room) > LIST, jnp.max(count) > CAP).astype(jnp.int32)
        own_pos = jnp.where(open_ > 0, place.astype(jnp.int32) + runs[:, None], -1)
        own_pos = jnp.concatenate(
            [
                own_pos,
                jnp.pad(jnp.minimum(runs, LIST), (0, tokens - blocks))[None],
                jnp.broadcast_to(over, (6 - blocks % 8 + 1, tokens)),
            ]
        )
        order = (0, 1, 3, 2)

        def from_line(a, far):
            return lax.ppermute(a, "x", [(x, (x - far) % sx) for x in range(sx)])

        places = [own_pos] + [from_line(own_pos, far) for far in range(1, sx)]
        places = jnp.stack(places)
        pay = lax.all_to_all(jnp.broadcast_to(pay[None], (sz, *pay.shape)), "z", 0, 0, tiled=True)
        here, row, core = (lax.axis_index(name).astype(jnp.int32) for name in ("x", "y", "c"))
        meta = jnp.stack([core] + [(row + step - 2 * here) % sx for step in order] + [core] * 3)
        meta = jnp.concatenate([meta, places[:, blocks, :16].reshape(-1)])
        place_of = (row * sz + lax.axis_index("z")) * sc + core
        target = sampled - place_of * width

        def run(steps, mine, others):
            return partial_logits(meta, places, steps, mine, others, head_t, head_s)

        other = other_core(pay)
        after, ahead = neighbours(pay)
        part, stud0 = run((0,), [pay], [other])
        got = [to_owner(part, order[0])]
        far = opposite(pay)
        part, stud1 = run((1,), [after], [other_core(after)])
        got.append(to_owner(part, order[1]))
        part, stud3 = run((2,), [ahead], [other_core(ahead)])
        got.append(to_owner(part, order[2]))
        part, stud2 = run((3,), [far], [other_core(far)])
        got.append(to_owner(part, order[3]))

        early = early_sum(meta, blocks, got[:3])
        logits, stats = row_stats(meta, own_pos, target[None], places, early, got[3])
        grad, rows = row_grads(meta, own_pos, everyone(stats), logits)
        grads = [grad] + [from_line(grad, far) for far in range(1, sx)]
        head = head_gradient(meta, places, grads, [stud0, stud1, stud3, stud2], blocks)
        start = (rows[2, 0] > 0.5 * OVER, rows[0], rows[1], head)
        pays = {0: pay, 1: after, 3: ahead, 2: far}

        def redo(_):
            return (False, *dense(pays, head_t, head_s, allowed, target))

        return lax.while_loop(lambda held: held[0], redo, start)[1:]

    return per_device


def solution(mesh, sizes=(4, 8, 2)):
    sx, sz, sc = sizes
    grid = Mesh(mesh.devices.reshape(sx, sx, sz, sc), ("x", "y", "z", "c"))
    both = P("x", LOCAL)
    return jax.shard_map(
        build(sx, sz, sc),
        mesh=grid,
        in_specs=(both, both, both, both, both, P("x")),
        out_specs=(P("x"), P("x"), both),
        check_vma=False,
    )
```

```python
import functools

import jax
import jax.numpy as jnp
from jax import lax
from jax.experimental import pallas as pl
from jax.experimental.pallas import tpu as pltpu
from jax.sharding import Mesh
from jax.sharding import PartitionSpec as P

CAP = 80
LIST = 512
STARTS = 8
NEG = -1e30
OVER = 1e30
BLOCK = 128
LOCAL = ("y", "z", "c")


def dot(a, b, dims):
    return lax.dot_general(a, b, (dims, ((), ())), preferred_element_type=jnp.float32)


def params(**kw):
    return pltpu.CompilerParams(vmem_limit_bytes=36 << 20, **kw)


def window(meta, held, b):
    run = meta[STARTS + held * 16 + b]
    start = pl.multiple_of(jnp.minimum(run, LIST - CAP), 16)
    return start, pl.ds(start, CAP), run - start


def selector(pos_row, start):
    lines = lax.broadcasted_iota(jnp.int32, (CAP, pos_row.shape[-1]), 0)
    return lines + start == pos_row


def from_row(first):
    return lax.broadcasted_iota(jnp.int32, (CAP, BLOCK), 0) >= first


def diagonal():
    rows = lax.broadcasted_iota(jnp.int32, (CAP, BLOCK), 0)
    return rows == lax.broadcasted_iota(jnp.int32, (CAP, BLOCK), 1)


def coded(logits):
    peak = jnp.max(jnp.abs(logits), axis=1, keepdims=True)
    power = jnp.floor(jnp.log2(jnp.maximum(peak, 1e-30)))
    scaled = jnp.round(logits * jnp.exp2(14.0 - power))
    values = jnp.clip(scaled, -32767.0, 32767.0).astype(jnp.int32)
    return values, jnp.sum(jnp.where(diagonal(), power, 0.0), axis=0, keepdims=True)


def decoded(values, powers):
    power = jnp.sum(jnp.where(diagonal(), powers, 0.0), axis=1, keepdims=True)
    return values.astype(jnp.int32).astype(jnp.float32) * jnp.exp2(power - 14.0)


def partial_kernel(steps, meta, pos, *refs):
    count = len(steps)
    mine, others = refs[:count], refs[count : 2 * count]
    far_t, far_s = refs[2 * count : 2 * count + 2]
    outs = refs[2 * count + 2 : 3 * count + 2]
    kept, sel, rows_t, rows_s, powers, head_t, head_s, sems = refs[3 * count + 2 :]
    fetch_t = pltpu.make_async_copy(far_t, head_t, sems.at[0])
    fetch_s = pltpu.make_async_copy(far_s, head_s, sems.at[1])
    fetch_t.start()
    fetch_s.start()
    blocks = far_t.shape[1] // BLOCK
    depth, tokens = mine[0].shape[0], sel.shape[1]
    both = kept.shape[1] // depth
    first = meta[0] == 0
    powers[...] = jnp.zeros_like(powers)
    for i in range(count):
        held = meta[1 + steps[i]]
        sel[...] = jnp.zeros_like(sel)
        for k in range(blocks):
            start, here, _ = window(meta, held, k)
            mark = selector(pos[held, k : k + 1, :], start).astype(jnp.float32)
            sel[here, :] = (sel[here, :].astype(jnp.float32) + mark).astype(jnp.bfloat16)

        def chunk(z, _, i=i):
            a, o = mine[i][z, :tokens, :], others[i][z, :tokens, :]
            pair = jnp.concatenate([jnp.where(first, a, o), jnp.where(first, o, a)], axis=1)
            rows_t[i, :, pl.ds(pl.multiple_of(z * 256, 256), 256)] = dot(
                sel[...], pair, ((1,), (0,))
            ).astype(jnp.bfloat16)
            a = mine[i][z, tokens:, :].astype(jnp.float32)
            o = others[i][z, tokens:, :].astype(jnp.float32)
            parts = []
            for part in (jnp.where(first, a, o), jnp.where(first, o, a)):
                parts.append(jnp.concatenate([part[: both // 2], part[both // 2 :]], axis=1))
            kept[i, pl.ds(pl.multiple_of(z * both, 16), both), :] = jnp.concatenate(
                parts, axis=0
            ).astype(jnp.bfloat16)
            return 0

        lax.fori_loop(0, depth, chunk, 0)
        deep_s = kept.shape[1]
        for at in range(0, deep_s, 256):
            end = min(at + 256, deep_s)
            rows_s[i, :, at:end] = dot(sel[...], kept[i, at:end, :], ((1,), (1,))).astype(
                jnp.bfloat16
            )

    def two_blocks(b, _):
        columns = pl.ds(pl.multiple_of(b * 2 * BLOCK, 2 * BLOCK), 2 * BLOCK)
        runs = [
            [window(meta, meta[1 + steps[i]], 2 * b + k) for k in range(2)] for i in range(count)
        ]
        for h, (rows, head) in enumerate(((rows_t, head_t), (rows_s, head_s))):
            lines = jnp.concatenate(
                [rows[i, runs[i][k][1], :] for i in range(count) for k in range(2)], axis=0
            )
            product = dot(lines, head[:, columns], ((1,), (0,)))
            for i in range(count):
                for k in range(2):
                    at = (2 * i + k) * CAP
                    values, power = coded(product[at : at + CAP, k * BLOCK : (k + 1) * BLOCK])
                    _, here, first = runs[i][k]
                    before = outs[i][0, h, here, :].astype(jnp.int32)
                    values = jnp.where(from_row(first), values, before)
                    outs[i][0, h, here, :] = values.astype(jnp.int16)
                    powers[2 * i + h, pl.ds(2 * b + k, 1), :] = power
        return 0

    fetch_t.wait()
    fetch_s.wait()
    lax.fori_loop(0, blocks // 2, two_blocks, 0)
    for i in range(count):
        for h in range(2):
            outs[i][0, h, LIST:, :] = powers[2 * i + h].astype(jnp.int32).astype(jnp.int16)


def partial_logits(meta, pos, steps, mine, others, head_t, head_s):
    count = len(steps)
    tokens = pos.shape[-1]
    deep_t, width = head_t.shape
    deep_s = head_s.shape[0]
    blocks = width // BLOCK
    coded_rows = LIST + 16
    return pl.pallas_call(
        functools.partial(partial_kernel, steps),
        name="partial_logits",
        in_specs=[pl.BlockSpec(memory_space=pltpu.SMEM)]
        + [pl.BlockSpec(memory_space=pltpu.VMEM)] * (2 * count + 1)
        + [pl.BlockSpec(memory_space=pl.ANY)] * 2,
        scratch_shapes=[
            pltpu.VMEM((LIST, tokens), jnp.bfloat16),
            pltpu.VMEM((count, LIST, deep_t), jnp.bfloat16),
            pltpu.VMEM((count, LIST, deep_s), jnp.bfloat16),
            pltpu.VMEM((2 * count, 16, BLOCK), jnp.float32),
            pltpu.VMEM(head_t.shape, head_t.dtype),
            pltpu.VMEM(head_s.shape, head_s.dtype),
            pltpu.SemaphoreType.DMA((2,)),
        ],
        out_shape=[jax.ShapeDtypeStruct((1, 2, coded_rows, BLOCK), jnp.int16)] * count
        + [jax.ShapeDtypeStruct((count, deep_s, tokens), jnp.bfloat16)],
        compiler_params=params(),
        cost_estimate=pl.CostEstimate(
            flops=8 * count * blocks * CAP * (deep_t + deep_s) * tokens,
            bytes_accessed=2 * (deep_t + deep_s) * (width + count * tokens),
            transcendentals=0,
        ),
    )(meta, pos, *mine, *others, head_t, head_s)


def spread(mark, line):
    return jnp.sum(jnp.where(mark, line, jnp.zeros_like(line)), axis=1, keepdims=True)


def fold(mark, column):
    return jnp.sum(jnp.where(mark, column, jnp.zeros_like(column)), axis=0, keepdims=True)


def unpacked(meta, ref, h, blocks):
    powers = ref[0, h, LIST:, :].astype(jnp.int32).astype(jnp.float32)
    return [
        decoded(ref[0, h, window(meta, 0, b)[1], :], powers[b : b + 1, :]) for b in range(blocks)
    ]


def early_kernel(meta, a0, a1, a2, total):
    blocks = total.shape[1]
    for h in range(2):
        parts = zip(*(unpacked(meta, a, h, blocks) for a in (a0, a1, a2)))
        for b, (x, y, z) in enumerate(parts):
            total[h, b] = x + y + z


def scalars_first(arrays):
    return [pl.BlockSpec(memory_space=pltpu.SMEM)] + [
        pl.BlockSpec(memory_space=pltpu.VMEM)
    ] * arrays


def early_sum(meta, blocks, parts):
    return pl.pallas_call(
        early_kernel,
        name="early_sum",
        in_specs=scalars_first(3),
        out_shape=jax.ShapeDtypeStruct((2, blocks, CAP, BLOCK), jnp.float32),
        compiler_params=params(),
    )(meta, *parts)


def packed(top_t, sum_t, cross, top_s, sum_s, picked, over):
    some = sum_t > 0.0
    safe_t, safe_s = jnp.where(some, sum_t, 1.0), jnp.where(some, sum_s, 1.0)
    lse_t = jnp.where(some, top_t + jnp.log(safe_t), NEG)
    lse_s = jnp.where(some, top_s + jnp.log(safe_s), NEG)
    lines = [jnp.where(over, OVER, lse_t), jnp.where(some, cross / safe_t, 0.0), lse_s, picked]
    half = picked.shape[-1] // 2
    return jnp.concatenate([part for a in lines for part in (a[:, :half], a[:, half:])], axis=0)


def stats_kernel(meta, pos, target, places, early, last, logits, stats):
    blocks = logits.shape[1]
    tokens = pos.shape[-1]
    tops = [jnp.full((1, tokens), NEG, jnp.float32) for _ in range(2)]
    for h in range(2):
        for b, part in enumerate(unpacked(meta, last, h, blocks)):
            total = early[h, b] + part
            logits[h, b] = total
            peak = jnp.max(total, axis=1, keepdims=True)
            mark = selector(pos[b : b + 1, :], window(meta, 0, b)[0])
            tops[h] = jnp.maximum(
                tops[h], jnp.max(jnp.where(mark, peak, NEG), axis=0, keepdims=True)
            )
    zero = jnp.zeros((1, tokens), jnp.float32)
    sum_t, cross, sum_s, picked = zero, zero, zero, zero
    lanes = lax.broadcasted_iota(jnp.int32, (CAP, BLOCK), 1)
    for b in range(blocks):
        mark = selector(pos[b : b + 1, :], window(meta, 0, b)[0])
        lt, ls = logits[0, b], logits[1, b]
        et = jnp.exp(lt - spread(mark, tops[0]))
        es = jnp.exp(ls - spread(mark, tops[1]))
        wanted = spread(mark, target[...] - b * BLOCK)
        sum_t = sum_t + fold(mark, jnp.sum(et, axis=1, keepdims=True))
        cross = cross + fold(mark, jnp.sum(et * (lt - ls), axis=1, keepdims=True))
        sum_s = sum_s + fold(mark, jnp.sum(es, axis=1, keepdims=True))
        picked = picked + fold(
            mark, jnp.sum(jnp.where(lanes == wanted, ls, 0.0), axis=1, keepdims=True)
        )
    over = jnp.max(jnp.concatenate([places[t, 11:12, :] for t in range(4)]), axis=0, keepdims=True)
    stats[...] = packed(tops[0], sum_t, cross, tops[1], sum_s, picked, over > 0)


def row_stats(meta, pos, target, places, early, last):
    return pl.pallas_call(
        stats_kernel,
        name="row_stats",
        in_specs=scalars_first(5),
        out_shape=[
            jax.ShapeDtypeStruct(early.shape, jnp.float32),
            jax.ShapeDtypeStruct((8, pos.shape[-1] // 2), jnp.float32),
        ],
        compiler_params=params(),
    )(meta, pos, target, places, early, last)


def combined(seen):
    lse_t, ratio, lse_s, picked = (
        jnp.concatenate([seen[:, 2 * k, :], seen[:, 2 * k + 1, :]], axis=1) for k in range(4)
    )
    total = lambda a: jnp.sum(a, axis=0, keepdims=True)
    top_t = jnp.max(lse_t, axis=0, keepdims=True)
    top_s = jnp.max(lse_s, axis=0, keepdims=True)
    share_t = jnp.exp(lse_t - top_t)
    sum_t = total(share_t)
    log_t = top_t + jnp.log(sum_t)
    log_s = top_s + jnp.log(total(jnp.exp(lse_s - top_s)))
    row_kl = total(share_t * ratio) / sum_t - log_t + log_s
    return log_t, log_s, row_kl, total(picked) - log_s, top_t


def grad_kernel(meta, pos, seen, logits, grad, rows, lines):
    log_t, log_s, row_kl, logprob, top = combined(seen[...])
    rows[...] = jnp.concatenate([row_kl, logprob, top] + [top] * 5, axis=0)
    lines[...] = jnp.zeros_like(lines)
    for b in range(logits.shape[1]):
        start, here, first = window(meta, 0, b)
        mark = selector(pos[b : b + 1, :], start)
        et = jnp.exp(logits[0, b] - spread(mark, log_t))
        es = jnp.exp(logits[1, b] - spread(mark, log_s))
        own = jnp.where(spread(mark, jnp.ones_like(log_t)) > 0.0, es - et, 0.0)
        lines[here, :] = jnp.where(from_row(first), own, lines[here, :])
    grad[...] = lines[...].astype(jnp.bfloat16)


def row_grads(meta, pos, seen, logits):
    return pl.pallas_call(
        grad_kernel,
        name="row_grads",
        in_specs=scalars_first(3),
        out_shape=[
            jax.ShapeDtypeStruct((LIST, BLOCK), jnp.bfloat16),
            jax.ShapeDtypeStruct((8, pos.shape[-1]), jnp.float32),
        ],
        scratch_shapes=[pltpu.VMEM((LIST, BLOCK), jnp.float32)],
        compiler_params=params(),
    )(meta, pos, seen, logits)


def scattered(meta, places, grad, t, pair):
    sides = []
    for k in range(2):
        start, here, _ = window(meta, t, 2 * pair + k)
        mark = selector(places[t, 2 * pair + k][None], start).astype(jnp.float32)
        mark = mark.astype(jnp.bfloat16)
        sides.append(dot(mark, grad[here, :], ((0,), (0,))).astype(jnp.bfloat16))
    return jnp.concatenate(sides, axis=1)


def own_head_kernel(meta, places, grad, *refs):
    *studs, left, base = refs
    tokens = places.shape[-1]
    for step, ref in enumerate(studs):
        at = pl.multiple_of(meta[1 + step] * tokens, tokens)
        left[:, pl.ds(at, tokens)] = ref[0]

    def pair(b, _):
        columns = pl.ds(pl.multiple_of(b * 2 * BLOCK, 2 * BLOCK), 2 * BLOCK)
        right = scattered(meta, places, grad, 0, b)
        base[:, columns] = dot(left[:, :tokens], right, ((1,), (0,)))
        return 0

    lax.fori_loop(0, base.shape[1] // (2 * BLOCK), pair, 0)


def own_head(meta, places, grad, studs, blocks):
    deep, tokens = studs[0].shape[1:]
    return pl.pallas_call(
        own_head_kernel,
        name="own_head",
        in_specs=scalars_first(2 + len(studs)),
        out_shape=[
            jax.ShapeDtypeStruct((deep, len(studs) * tokens), jnp.bfloat16),
            jax.ShapeDtypeStruct((deep, blocks * BLOCK), jnp.float32),
        ],
        compiler_params=params(),
        cost_estimate=pl.CostEstimate(
            flops=2 * deep * tokens * blocks * BLOCK,
            bytes_accessed=deep * (4 * tokens + 4 * blocks * BLOCK),
            transcendentals=0,
        ),
    )(meta, places, grad, *studs)


def head_kernel(meta, places, left, base, *refs):
    *grads, out = refs
    tokens = places.shape[-1]
    b = pl.program_id(0)
    right = [scattered(meta, places, grad, t + 1, b) for t, grad in enumerate(grads)]
    out[...] = base[...] + dot(left[:, tokens:], jnp.concatenate(right, axis=0), ((1,), (0,)))


def head_gradient(meta, places, left, base, grads):
    deep, width = base.shape
    whole = lambda a: pl.BlockSpec(a.shape, lambda b, meta: (0,) * a.ndim)
    columns = pl.BlockSpec((deep, 2 * BLOCK), lambda b, meta: (0, b))
    return pl.pallas_call(
        head_kernel,
        name="head_gradient",
        grid_spec=pltpu.PrefetchScalarGridSpec(
            num_scalar_prefetch=1,
            grid=(width // (2 * BLOCK),),
            in_specs=[whole(places), whole(left), columns] + [whole(a) for a in grads],
            out_specs=columns,
        ),
        out_shape=jax.ShapeDtypeStruct((deep, width), jnp.float32),
        compiler_params=params(),
    )(meta, places, left, base, *grads)


def build(sx, sz, sc):
    turn = lambda step: [
        (x * sx + y, ((y + step - x) % sx) * sx + y) for x in range(sx) for y in range(sx)
    ]
    spread_out = [(x * sx + y, y * sx + (x + y) % sx) for x in range(sx) for y in range(sx)]
    shift = lambda step: [(y, (y + step) % sx) for y in range(sx)]

    def to_owner(a, step):
        return lax.ppermute(a, ("x", "y"), turn(step))

    def both_cores(mine):
        if sc == 1:
            return mine[:, None]
        other = lax.ppermute(mine, "c", [(0, 1), (1, 0)])
        first = lax.axis_index("c") == 0
        return jnp.stack([jnp.where(first, mine, other), jnp.where(first, other, mine)], axis=1)

    def features(pay, tokens):
        full = both_cores(pay)
        chunks = full.shape[0] * full.shape[1]
        full = full.reshape(chunks, -1, BLOCK)
        teach = full[:, :tokens]
        stud = full[:, tokens:].reshape(chunks, tokens // BLOCK, -1, BLOCK)
        stud = stud.transpose(0, 2, 1, 3).reshape(-1, tokens)
        return teach, stud

    def neighbours(pay):
        after = lax.ppermute(pay, "y", shift(-1))
        before = lax.ppermute(pay, "y", shift(1))
        return after, before

    def opposite(pay):
        return lax.ppermute(pay, "y", shift(2))

    def everyone(stats):
        copies = jnp.broadcast_to(stats[None], (sx * sz * sc, *stats.shape))
        return lax.all_to_all(copies, LOCAL, split_axis=0, concat_axis=0, tiled=True)

    def dense(pays, head_t, head_s, allowed, target):
        tokens, blocks = allowed.shape
        width = head_t.shape[1]
        pairs = [features(pays[step], tokens) for step in range(sx)]
        teach = jnp.concatenate([t.transpose(1, 0, 2).reshape(tokens, -1) for t, _ in pairs])
        studs = jnp.concatenate([stud for _, stud in pairs], axis=1)
        part = jnp.concatenate(
            [dot(teach, head_t, ((1,), (0,))), dot(studs, head_s, ((0,), (0,)))], axis=1
        )
        total = sum(
            to_owner(part[step * tokens : (step + 1) * tokens], step) for step in range(sx)
        )
        lt, ls = total[:, :width], total[:, width:]
        open_ = jnp.broadcast_to((allowed > 0)[:, :, None], (tokens, blocks, BLOCK))
        open_ = open_.reshape(tokens, width)
        ids = jnp.arange(width, dtype=jnp.int32)
        picked = jnp.sum(jnp.where(ids[None, :] == target[:, None], ls, 0.0), axis=1)
        top_t = jnp.max(jnp.where(open_, lt, NEG), axis=1)
        top_s = jnp.max(jnp.where(open_, ls, NEG), axis=1)
        et = jnp.where(open_, jnp.exp(jnp.where(open_, lt, NEG) - top_t[:, None]), 0.0)
        es = jnp.where(open_, jnp.exp(jnp.where(open_, ls, NEG) - top_s[:, None]), 0.0)
        lines = [top_t, et.sum(1), (et * (lt - ls)).sum(1), top_s, es.sum(1), picked]
        stats = packed(*(line[None] for line in lines), False)
        log_t, log_s, row_kl, logprob, _ = combined(everyone(stats))
        scale_t = jnp.exp(top_t - log_t[0])
        scale_s = jnp.exp(top_s - log_s[0])
        grad = (es * scale_s[:, None] - et * scale_t[:, None]).astype(jnp.bfloat16)
        grads = jnp.concatenate([to_owner(grad, step) for step in range(sx)])
        head = dot(studs, grads, ((1,), (0,)))
        return row_kl[0], logprob[0], head

    def other_core(pay):
        return lax.ppermute(pay, "c", [(0, 1), (1, 0)]) if sc > 1 else pay

    def per_device(teacher_hidden, student_hidden, head_t, head_s, allowed, sampled):
        tokens, blocks = allowed.shape
        width = head_t.shape[1]
        stud = student_hidden.T.reshape(-1, tokens // BLOCK, BLOCK).transpose(1, 0, 2)
        pay = jnp.concatenate([teacher_hidden, stud.reshape(-1, BLOCK)], axis=0)
        pay = lax.ppermute(pay, ("x", "y"), spread_out)
        open_ = (allowed > 0).T.astype(jnp.float32)
        before = jnp.triu(jnp.ones((tokens, tokens), jnp.float32), 1)
        place = dot(open_.astype(jnp.bfloat16), before.astype(jnp.bfloat16), ((1,), (0,)))
        count = jnp.sum(open_, axis=1).astype(jnp.int32)
        room = (count + 15) // 16 * 16
        ahead_of = jnp.arange(blocks)[None, :] < jnp.arange(blocks)[:, None]
        runs = jnp.sum(jnp.where(ahead_of, room[None, :], 0), axis=1)
        over = jnp.logical_or(jnp.sum(room) > LIST, jnp.max(count) > CAP).astype(jnp.int32)
        own_pos = jnp.where(open_ > 0, place.astype(jnp.int32) + runs[:, None], -1)
        own_pos = jnp.concatenate(
            [
                own_pos,
                jnp.pad(jnp.minimum(runs, LIST), (0, tokens - blocks))[None],
                jnp.broadcast_to(over, (6 - blocks % 8 + 1, tokens)),
            ]
        )
        order = (0, 1, 3, 2)

        def from_line(a, far):
            return lax.ppermute(a, "x", [(x, (x - far) % sx) for x in range(sx)])

        places = [own_pos] + [from_line(own_pos, far) for far in range(1, sx)]
        places = jnp.stack(places)
        pay = lax.all_to_all(jnp.broadcast_to(pay[None], (sz, *pay.shape)), "z", 0, 0, tiled=True)
        here, row, core = (lax.axis_index(name).astype(jnp.int32) for name in ("x", "y", "c"))
        meta = jnp.stack([core] + [(row + step - 2 * here) % sx for step in order] + [core] * 3)
        meta = jnp.concatenate([meta, places[:, blocks, :16].reshape(-1)])
        place_of = (row * sz + lax.axis_index("z")) * sc + core
        target = sampled - place_of * width

        def run(steps, mine, others):
            return partial_logits(meta, places, steps, mine, others, head_t, head_s)

        other = other_core(pay)
        after, ahead = neighbours(pay)
        part, stud0 = run((0,), [pay], [other])
        got = [to_owner(part, order[0])]
        far = opposite(pay)
        part, stud1 = run((1,), [after], [other_core(after)])
        got.append(to_owner(part, order[1]))
        part, stud3 = run((2,), [ahead], [other_core(ahead)])
        got.append(to_owner(part, order[2]))
        part, stud2 = run((3,), [far], [other_core(far)])
        got.append(to_owner(part, order[3]))

        early = early_sum(meta, blocks, got[:3])
        logits, stats = row_stats(meta, own_pos, target[None], places, early, got[3])
        grad, rows = row_grads(meta, own_pos, everyone(stats), logits)
        grads = [from_line(grad, far) for far in range(1, sx)]
        left, base = own_head(meta, places, grad, [stud0, stud1, stud3, stud2], blocks)
        head = head_gradient(meta, places, left, base, grads)
        start = (rows[2, 0] > 0.5 * OVER, rows[0], rows[1], head)
        pays = {0: pay, 1: after, 3: ahead, 2: far}

        def redo(_):
            return (False, *dense(pays, head_t, head_s, allowed, target))

        return lax.while_loop(lambda held: held[0], redo, start)[1:]

    return per_device


def solution(mesh, sizes=(4, 8, 2)):
    sx, sz, sc = sizes
    grid = Mesh(mesh.devices.reshape(sx, sx, sz, sc), ("x", "y", "z", "c"))
    both = P("x", LOCAL)
    return jax.shard_map(
        build(sx, sz, sc),
        mesh=grid,
        in_specs=(both, both, both, both, both, P("x")),
        out_specs=(P("x"), P("x"), both),
        check_vma=False,
    )
```
